32 devices in a mesh: groups: 2 (over y), seq: 16 (over z, x, core).
Axes of the slice: x: 2, y: 2, z: 4, core: 2. Of those that a mesh axis runs over, the one named last changes fastest.
Arguments:
- queries: bfloat16 [4096, 1536], P(('groups', 'seq')), parts along dimension 0, may hold values from -6 to 6
- keys: bfloat16 [4096, 1536], P(('groups', 'seq')), parts along dimension 0, may hold values from -6 to 6
- values: bfloat16 [4096, 1536], P(('groups', 'seq')), parts along dimension 0, may hold values from -6 to 6
- w_out: bfloat16 [1536, 3072], replicated, may hold values from -0.15625 to 0.15625
- shift_mod: float32 [6144], P('groups'), parts along dimension 0, may hold values from -5 to 5
- scale_mod: float32 [6144], P('groups'), parts along dimension 0, may hold values from -3 to 3
- w_final: bfloat16 [3072, 64], replicated, may hold values from -0.109375 to 0.109375
- conv_weight: bfloat16 [432, 512], replicated, may hold values from -0.3125 to 0.3125
- conv_bias: float32 [512], replicated, may hold values from -3 to 3
Outputs:
- decoded: bfloat16 [8, 32, 64, 512], P('groups', 'seq'), parts along dimension 0
The draws below stay inside these ranges and needn't reach their ends.
There are 2 independent parts, one for each index of `groups`. The reference program is written for one: setup_inputs(seed, part) draws one part's arguments, and reference() takes and returns one part's arrays. A program takes and returns all parts, laid end to end along the dimension named above; an argument that names none is the same for every part. Nothing has to cross between parts.
All inputs are finite; a program needn't handle non-finite values.
Results may differ from the reference program's by a relative error of at most 0.018.
Values may be sent and summed in bfloat16 or wider, within the bound.
A program may use at most 192 MiB of HBM per device.

```python
import math
import jax
import jax.numpy as jnp
from jax import lax

D = 3072
HEADS = 12
HEAD_DIM = 128
LATENT_CH = 16
CONV_CH = 512
FRAMES = 4
ROWS = 32
TOKENS = 2048


def draw_queries(key, part):
    base = jnp.clip(jax.random.normal(jax.random.fold_in(key, 1), (TOKENS, HEADS * HEAD_DIM), jnp.float32), -6.0, 6.0)
    return base.astype(jnp.bfloat16)


def draw_keys(key, part):
    base = jnp.clip(jax.random.normal(jax.random.fold_in(key, 2), (TOKENS, HEADS * HEAD_DIM), jnp.float32), -6.0, 6.0)
    return base.astype(jnp.bfloat16)


def shard_levels(stream_key, dims, shards, smallest, high):
    factor_of, own = 1.0, jax.random.fold_in(stream_key, 6)
    for dim, blocks in shards:
        steps = jnp.exp(jax.random.uniform(jax.random.fold_in(own, dim), (blocks,), jnp.float32, smallest / len(shards), high / len(shards)))
        factor_of = factor_of * jnp.repeat(steps, dims[dim] // blocks).reshape([-1 if axis == dim else 1 for axis in range(len(dims))])
    return factor_of


def scatter_about(own_key, extent, scale, most, cuts=(), kind=jnp.bfloat16):
    drawn = scale * jax.random.normal(own_key, extent, jnp.float32)
    if cuts:
        drawn = drawn * shard_levels(own_key, extent, cuts, -0.22, 0.18)
    return jnp.clip(drawn, -most, most).astype(kind)


def setup_inputs(seed: int = 0, part: int = 0) -> dict:
    key_of = jax.random.split(jax.random.key(seed), 10)
    part_splits = jax.random.split(jax.random.fold_in(key_of[9], part), 10)
    queries = draw_queries(jax.random.fold_in(jax.random.fold_in(key_of[9], part), 71), part)
    keys = draw_keys(jax.random.fold_in(jax.random.fold_in(key_of[9], part), 71), part)
    values = scatter_about(part_splits[2], (TOKENS, HEADS * HEAD_DIM), 1.0, 6.0, ((0, 16),))
    w_out = scatter_about(key_of[3], (HEADS * HEAD_DIM, D), (HEADS * HEAD_DIM) ** -0.5, 0.15625)
    shift_mod = scatter_about(part_splits[4], (D,), 1.0, 5.0, (), jnp.float32)
    scale_mod = scatter_about(part_splits[5], (D,), 0.5, 3.0, (), jnp.float32)
    w_final = scatter_about(key_of[6], (D, 4 * LATENT_CH), D ** -0.5, 0.109375)
    conv_weight = scatter_about(key_of[7], (27 * LATENT_CH, CONV_CH), (27 * LATENT_CH) ** -0.5, 0.3125)
    conv_bias = scatter_about(key_of[8], (CONV_CH,), 0.5, 3.0, (), jnp.float32)
    return {"queries": queries, "keys": keys, "values": values, "w_out": w_out, "shift_mod": shift_mod, "scale_mod": scale_mod, "w_final": w_final, "conv_weight": conv_weight, "conv_bias": conv_bias}


def convolve(padded, conv_weight, conv_bias, frames, width, height):
    taps = []
    for shift_t in range(3):
        for shift_x in range(3):
            for shift_y in range(3):
                taps.append(padded[shift_t:shift_t + frames, shift_x:shift_x + width, shift_y:shift_y + height, :])
    stacked = jnp.concatenate(taps, axis=3)
    flat = stacked.reshape(frames * width * height, stacked.shape[3])
    output = jnp.dot(flat, conv_weight, preferred_element_type=jnp.float32) + conv_bias
    return output.astype(jnp.bfloat16).reshape(frames, width, height, conv_weight.shape[1])

def reference(queries, keys, values, w_out, shift_mod, scale_mod, w_final, conv_weight, conv_bias):
    tokens = queries.shape[0]
    inv_root = 1.0 / math.sqrt(HEAD_DIM)
    query_heads = queries.astype(jnp.float32).reshape(tokens, HEADS, HEAD_DIM).transpose(1, 0, 2)
    key_heads = keys.astype(jnp.float32).reshape(tokens, HEADS, HEAD_DIM).transpose(1, 0, 2)
    value_heads = values.reshape(tokens, HEADS, HEAD_DIM).transpose(1, 0, 2)
    block_rows = min(2048, tokens)

    def per_head(operands):
        query_h, key_h, value_h = operands

        def per_block(query_b):
            scores = jnp.dot(query_b, key_h.T, precision=lax.Precision.HIGHEST) * inv_root
            peak = lax.optimization_barrier(jnp.max(scores, axis=1, keepdims=True))
            exp_scores = jnp.exp(scores - peak)
            weights = lax.optimization_barrier(exp_scores.astype(jnp.bfloat16))
            summed = jnp.dot(weights, value_h, preferred_element_type=jnp.float32)
            return (summed / lax.optimization_barrier(jnp.sum(exp_scores, axis=1, keepdims=True))).astype(jnp.bfloat16)
        query_blocks = query_h.reshape(tokens // block_rows, block_rows, HEAD_DIM)
        return lax.map(per_block, query_blocks).reshape(tokens, HEAD_DIM)
    attended = lax.map(per_head, (query_heads, key_heads, value_heads))
    attended = attended.transpose(1, 0, 2).reshape(tokens, HEADS * HEAD_DIM)
    projected = jnp.dot(attended, w_out, preferred_element_type=jnp.float32)
    centered = projected - lax.optimization_barrier(jnp.mean(projected, axis=1, keepdims=True))
    variance = lax.optimization_barrier(jnp.mean(centered * centered, axis=1, keepdims=True))
    normed = (centered * lax.rsqrt(variance + 1e-06) * (1.0 + scale_mod) + shift_mod).astype(jnp.bfloat16)
    patches = jnp.dot(normed, w_final, preferred_element_type=jnp.float32).astype(jnp.bfloat16)
    columns = tokens // (FRAMES * ROWS)
    latent = patches.reshape(FRAMES, ROWS, columns, LATENT_CH, 2, 2).transpose(0, 2, 5, 1, 4, 3)
    latent = latent.reshape(FRAMES, 2 * columns, 2 * ROWS, LATENT_CH)
    padded = jnp.pad(latent, ((2, 0), (1, 1), (1, 1), (0, 0)), mode='edge')
    return convolve(padded, conv_weight, conv_bias, FRAMES, 2 * columns, 2 * ROWS)
```

```python
import functools
import math

import jax
import jax.numpy as jnp
from jax import lax
from jax.experimental import pallas as pl
from jax.experimental.pallas import tpu as pltpu
from jax.sharding import PartitionSpec as P

HEADS = 12
HEAD_DIM = 128
QUAD = 4
OWNERS = 3
CHUNK = 2048
LATENT_CH = 16
FRAMES = 4
ROWS = 32
BF = jnp.bfloat16
F32 = jnp.float32


def mm(a, b):
    return lax.dot_general(a, b, (((1,), (0,)), ((), ())), preferred_element_type=F32)


def iota(shape, dim):
    return lax.broadcasted_iota(jnp.int32, shape, dim)


def ones_where(cond):
    return jnp.where(cond, 1.0, 0.0).astype(BF)


def kernel(
    n, split,
    q_hbm, k_hbm, v_hbm, w_out_hbm, shift_ref, scale_ref, w_final_hbm,
    out_ref,
    qb, kb, vb, ob, att, w_out_v, w_final_v, proj, send_b, recv_b,
    s_send, kv_recv, q_recv, o_send, o_recv, e_send, e_recv, loc,
):
    me = lax.axis_index("seq")
    grp = me // QUAD
    tok = q_hbm.shape[0]
    rows_dev = tok // n
    groups = n // QUAD
    nq = n // split
    quads = nq // QUAD

    def cols(h):
        return pl.ds(pl.multiple_of(h * HEAD_DIM, 128), HEAD_DIM)

    def remote(src, dst, ssem, rsem, dev):
        return pltpu.make_async_remote_copy(
            src_ref=src, dst_ref=dst, send_sem=ssem, recv_sem=rsem,
            device_id={"seq": dev}, device_id_type=pl.DeviceIdType.MESH,
        )

    def arrived(ref, sem):
        pltpu.make_async_copy(ref, ref, sem).wait()

    def place(g, p):
        return g * QUAD + (p + 2 * (g % 2)) % QUAD

    mine = (me % QUAD + QUAD - 2 * (grp % 2)) % QUAD
    unit = grp * OWNERS + mine
    head = unit // split
    origin = (unit % split) * nq

    barrier = pltpu.get_barrier_semaphore()

    def greet(i, c):
        pl.semaphore_signal(
            barrier, inc=1, device_id={"seq": (me + i) % n}, device_id_type=pl.DeviceIdType.MESH
        )
        return c

    lax.fori_loop(1, n, greet, 0)
    pl.semaphore_wait(barrier, n - 1)

    raw = (q_hbm, k_hbm, v_hbm)
    bufs = (qb, kb, vb)

    def target(i):
        g = grp ^ (groups - 1 - i // OWNERS)
        p = i % OWNERS
        return g * OWNERS + p, place(g, p)

    def push(t, u, dev):
        src = raw[t].at[:, cols(u // split)]
        slot = me % nq if t == 0 else me
        sem = q_recv.at[slot] if t == 0 else kv_recv.at[t - 1]

        @pl.when(dev != me)
        def _():
            remote(src, bufs[t].at[slot], s_send.at[t, u], sem, dev).start()

        @pl.when(dev == me)
        def _():
            pltpu.make_async_copy(src, bufs[t].at[slot], sem).start()

    def push_kv(i, c):
        u, dev = target(i)
        push(1, u, dev)
        push(2, u, dev)
        return c

    def push_q(i, c):
        u, dev = target(i)

        @pl.when(u % split == me // nq)
        def _():
            push(0, u, dev)

        return c

    lax.fori_loop(0, groups * OWNERS, push_kv, 0)
    lax.fori_loop(0, groups * OWNERS, push_q, 0)
    w_out_copy = pltpu.make_async_copy(w_out_hbm, w_out_v, loc.at[0])
    w_final_copy = pltpu.make_async_copy(w_final_hbm, w_final_v, loc.at[1])
    w_out_copy.start()
    w_final_copy.start()

    def far_order(i, quads):
        k = quads - 1 - i
        z = grp % quads
        outer = (z % 2) == (z // (quads // 2))
        return z ^ jnp.where(outer & (k >= 2), k ^ 1, k)

    factor = math.log2(math.e) / math.sqrt(HEAD_DIM)
    keys = n * tok
    chunk = min(keys, CHUNK)
    pair = 2 * tok

    def scores(qh, c):
        kh = kb[pl.ds(c * (chunk // tok), chunk // tok)].reshape(chunk, HEAD_DIM)
        s = lax.dot_general(qh, kh, (((1,), (1,)), ((), ())), preferred_element_type=F32)
        return s * factor

    def weigh(s, top, c):
        vh = vb[pl.ds(c * (chunk // tok), chunk // tok)].reshape(chunk, HEAD_DIM)
        p = jnp.exp2(s - top).astype(BF)
        return mm(p, jnp.concatenate([vh, jnp.ones((chunk, HEAD_DIM), BF)], axis=1))

    def attend(i, carry):
        slot = QUAD * far_order(i // 2, quads) + 2 * (i % 2)
        for e in range(2):
            arrived(qb.at[slot + e], q_recv.at[slot + e])
        qh = qb[pl.ds(slot, 2)].reshape(pair, HEAD_DIM)
        if chunk == keys:
            s = scores(qh, 0)
            acc = weigh(s, jnp.max(s, axis=1, keepdims=True), 0)
        else:

            def step(c, state):
                top, acc = state
                s = scores(qh, c)
                new = jnp.maximum(top, jnp.max(s, axis=1, keepdims=True))
                return new, acc * jnp.exp2(top - new) + weigh(s, new, c)

            first = jnp.full((pair, 1), -1e30, F32), jnp.zeros((pair, 2 * HEAD_DIM), F32)
            acc = lax.fori_loop(0, keys // chunk, step, first)[1]
        ob[pl.ds(slot, 2)] = (acc[:, :HEAD_DIM] / acc[:, HEAD_DIM:]).astype(BF).reshape(2, tok, HEAD_DIM)
        for e in range(2):
            dev = origin + slot + e

            @pl.when(dev != me)
            def _(e=e, dev=dev):
                remote(ob.at[slot + e], att.at[head], o_send.at[slot + e], o_recv.at[head], dev).start()

            @pl.when(dev == me)
            def _(e=e):
                pltpu.make_async_copy(ob.at[slot + e], att.at[head], o_recv.at[head]).start()

        return carry

    @pl.when(mine < OWNERS)
    def _():
        arrived(kb, kv_recv.at[0])
        arrived(vb, kv_recv.at[1])
        lax.fori_loop(0, nq // 2, attend, 0)

    def sent(i, c):
        u, dev = target(i)
        for t in range(3):
            slot = me % nq if t == 0 else me

            @pl.when((dev != me) & ((t > 0) | (u % split == me // nq)))
            def _(t=t, slot=slot):
                remote(raw[t].at[:, cols(u // split)], bufs[t].at[slot], s_send.at[t, u], e_recv.at[0], dev).wait_send()

        return c

    lax.fori_loop(0, groups * OWNERS, sent, 0)
    w_out_copy.wait()
    for i in range(HEADS // OWNERS):
        first = OWNERS * far_order(HEADS // OWNERS - 1 - i, HEADS // OWNERS)
        for e in range(OWNERS):
            arrived(att.at[first + e], o_recv.at[first + e])
        lhs = jnp.concatenate([att[first + e] for e in range(OWNERS)], axis=1)
        rows = pl.ds(pl.multiple_of(first * HEAD_DIM, OWNERS * HEAD_DIM), OWNERS * HEAD_DIM)
        term = mm(lhs, w_out_v[rows])
        proj[...] = term if i == 0 else proj[...] + term
    projected = proj[...]
    centered = projected - jnp.mean(projected, axis=1, keepdims=True)
    variance = jnp.mean(centered * centered, axis=1, keepdims=True)
    normed = (
        centered * lax.rsqrt(variance + 1e-06) * (1.0 + scale_ref[...]) + shift_ref[...]
    ).astype(BF)
    w_final_copy.wait()
    patches = lax.dot_general(
        normed, w_final_v[...], (((1,), (1,)), ((), ())), preferred_element_type=F32
    ).astype(BF)

    ch = iota((4 * LATENT_CH, 128), 0)
    lane = iota((4 * LATENT_CH, 128), 1)
    base = 4 * (lane % 16) + 2 * (lane // 64)
    xcol = (lane // 16) % 4
    row = iota((tok, tok), 0)
    col = iota((tok, tok), 1)
    w = row // rows_dev
    here = (row % rows_dev) * n + w
    picks = (
        ((col == here - 1) & (w > 0), (xcol == 0) & (ch == base + 1)),
        ((col == here) & (w == 0), (xcol == 0) & (ch == base)),
        (col == here, ((xcol == 1) & (ch == base)) | ((xcol == 2) & (ch == base + 1))),
        ((col == here + 1) & (w < n - 1), (xcol == 3) & (ch == base)),
        ((col == here) & (w == n - 1), (xcol == 3) & (ch == base + 1)),
    )
    window = None
    for rows_pick, ch_pick in picks:
        term = mm(ones_where(rows_pick), mm(patches, ones_where(ch_pick)).astype(BF))
        window = term if window is None else window + term
    send_b[...] = window.reshape(n, rows_dev, 128)

    def e_copy(i):
        dev = (me + i) % n
        return remote(send_b.at[dev], recv_b.at[me], e_send.at[i], e_recv.at[i], dev)

    def e_start(i, c):
        e_copy(i).start()
        return c

    def e_wait(i, c):
        src = (me + n - i) % n
        remote(recv_b.at[src], recv_b.at[src], e_send.at[i], e_recv.at[i], src).wait_recv()
        e_copy(i).wait_send()
        return c

    lax.fori_loop(1, n, e_start, 0)
    recv_b[me] = send_b[me]
    lax.fori_loop(1, n, e_wait, 0)

    def returned(slot, c):
        @pl.when(origin + slot != me)
        def _():
            remote(ob.at[slot], att.at[head], o_send.at[slot], e_recv.at[0], origin + slot).wait_send()

        return c

    @pl.when(mine < OWNERS)
    def _():
        lax.fori_loop(0, nq, returned, 0)

    out_ref[...] = recv_b[...].reshape(out_ref.shape)


def conv_kernel(got_ref, conv_v, bias_ref, out_ref, big_w):
    out_ch = conv_v.shape[1]
    big_w[...] = jnp.zeros(big_w.shape, BF)
    for a in range(3):
        for e in range(3):
            for b in range(3):
                for s in range(2):
                    big_w[
                        (a * 3 + e) * 64 + (b + s) * 16 : (a * 3 + e) * 64 + (b + s) * 16 + 16,
                        s * out_ch : (s + 1) * out_ch,
                    ] = conv_v[(9 * a + 3 * b + e) * 16 : (9 * a + 3 * b + e) * 16 + 16, :]
    got = got_ref[...]
    turned = pltpu.roll(got, 64, 1)
    low = iota(got.shape, 1) < 64
    lo = jnp.concatenate([jnp.where(low, got, 0.0), jnp.where(low, turned, 0.0)], axis=0).astype(BF)
    hi = jnp.concatenate([jnp.where(low, 0.0, turned), jnp.where(low, 0.0, got)], axis=0).astype(BF)
    cells = FRAMES * 2 * ROWS
    orow = iota((cells, cells), 0)
    ocol = iota((cells, cells), 1)
    of = orow // (2 * ROWS)
    oy = orow % (2 * ROWS)

    def pick(idx):
        a, e = idx // 3, idx % 3
        sf = jnp.maximum(of + (a - 2), 0)
        sy = jnp.clip(oy + (e - 1), 0, 2 * ROWS - 1)
        return ones_where(ocol == (sy % 2) * (FRAMES * ROWS) + sf * ROWS + sy // 2)

    feats = []
    for pair in range(5):
        x = mm(pick(2 * pair), lo)
        if 2 * pair + 1 < 9:
            x = x + mm(pick(2 * pair + 1), hi)
        feats.append(x.astype(BF))
    feats = jnp.concatenate(feats, axis=1)
    for s in range(2):
        res = mm(feats, big_w[:, s * out_ch : (s + 1) * out_ch]) + bias_ref[...]
        res = res.astype(BF)
        for f in range(FRAMES):
            out_ref[f, s] = res[f * 2 * ROWS : (f + 1) * 2 * ROWS]


def shards(queries, keys, values, w_out, shift_mod, scale_mod, w_final, conv_weight, conv_bias):
    n = lax.axis_size("seq")
    split = n * OWNERS // (QUAD * HEADS)
    tok = queries.shape[0]
    d = w_out.shape[1]
    out_ch = conv_weight.shape[1]
    vm = pl.BlockSpec(memory_space=pltpu.VMEM)
    hbm = pl.BlockSpec(memory_space=pltpu.HBM)
    dma = pltpu.SemaphoreType.DMA
    nq = n // split
    got = pl.pallas_call(
        functools.partial(kernel, n, split),
        out_shape=jax.ShapeDtypeStruct((FRAMES * ROWS, 128), F32),
        in_specs=[hbm, hbm, hbm, hbm, vm, vm, hbm],
        out_specs=vm,
        scratch_shapes=[
            pltpu.VMEM((nq, tok, HEAD_DIM), BF),
            pltpu.VMEM((n, tok, HEAD_DIM), BF),
            pltpu.VMEM((n, tok, HEAD_DIM), BF),
            pltpu.VMEM((nq, tok, HEAD_DIM), BF),
            pltpu.VMEM((HEADS, tok, HEAD_DIM), BF),
            pltpu.VMEM(w_out.shape, BF),
            pltpu.VMEM(w_final.shape[::-1], BF),
            pltpu.VMEM((tok, d), F32),
            pltpu.VMEM((n, tok // n, 128), F32),
            pltpu.VMEM((n, tok // n, 128), F32),
            dma((3, HEADS * split)), dma((2,)), dma((nq,)),
            dma((nq,)), dma((HEADS,)),
            dma((n,)), dma((n,)),
            dma((2,)),
        ],
        compiler_params=pltpu.CompilerParams(
            collective_id=0, has_side_effects=True, vmem_limit_bytes=56 * 1024 * 1024
        ),
        name="fused",
    )(
        queries, keys, values, w_out,
        shift_mod.reshape(1, d), scale_mod.reshape(1, d), w_final.T,
    )
    return pl.pallas_call(
        conv_kernel,
        out_shape=jax.ShapeDtypeStruct((FRAMES, 2, 2 * ROWS, out_ch), BF),
        in_specs=[vm, vm, vm],
        out_specs=vm,
        scratch_shapes=[pltpu.VMEM((640, 2 * out_ch), BF)],
        name="conv",
    )(got, conv_weight, conv_bias.reshape(1, out_ch))


def solution(mesh):
    placed = (
        P(("groups", "seq"), None),
        P(("groups", "seq"), None),
        P(("groups", "seq"), None),
        P(),
        P("groups"),
        P("groups"),
        P(),
        P(),
        P(),
    )
    return jax.shard_map(
        shards,
        mesh=mesh,
        in_specs=placed,
        out_specs=P("groups", "seq", None, None),
        check_vma=False,
    )
```

```python
import functools
import math

import jax
import jax.numpy as jnp
from jax import lax
from jax.experimental import pallas as pl
from jax.experimental.pallas import tpu as pltpu
from jax.sharding import PartitionSpec as P

HEADS = 12
HEAD_DIM = 128
QUAD = 4
OWNERS = 3
CHUNK = 2048
LATENT_CH = 16
FRAMES = 4
ROWS = 32
BF = jnp.bfloat16
F32 = jnp.float32


def mm(a, b):
    return lax.dot_general(a, b, (((1,), (0,)), ((), ())), preferred_element_type=F32)


def iota(shape, dim):
    return lax.broadcasted_iota(jnp.int32, shape, dim)


def ones_where(cond):
    return jnp.where(cond, 1.0, 0.0).astype(BF)


def kernel(
    n, split,
    q_hbm, k_hbm, v_hbm, w_out_hbm, shift_ref, scale_ref, w_final_hbm,
    out_ref,
    qb, kb, vb, ob, att, w_out_v, w_final_v, proj, send_b, recv_b,
    s_send, kv_recv, q_recv, o_send, o_recv, e_send, e_recv, loc,
):
    me = lax.axis_index("seq")
    grp = me // QUAD
    tok = q_hbm.shape[0]
    rows_dev = tok // n
    groups = n // QUAD
    nq = n // split
    quads = nq // QUAD

    def cols(h):
        return pl.ds(pl.multiple_of(h * HEAD_DIM, 128), HEAD_DIM)

    def remote(src, dst, ssem, rsem, dev):
        return pltpu.make_async_remote_copy(
            src_ref=src, dst_ref=dst, send_sem=ssem, recv_sem=rsem,
            device_id={"seq": dev}, device_id_type=pl.DeviceIdType.MESH,
        )

    def arrived(ref, sem):
        pltpu.make_async_copy(ref, ref, sem).wait()

    def place(g, p):
        return g * QUAD + (p + 2 * (g % 2)) % QUAD

    mine = (me % QUAD + QUAD - 2 * (grp % 2)) % QUAD
    unit = grp * OWNERS + mine
    head = unit // split
    origin = (unit % split) * nq

    barrier = pltpu.get_barrier_semaphore()

    def greet(i, c):
        pl.semaphore_signal(
            barrier, inc=1, device_id={"seq": (me + i) % n}, device_id_type=pl.DeviceIdType.MESH
        )
        return c

    lax.fori_loop(1, n, greet, 0)
    pl.semaphore_wait(barrier, n - 1)

    raw = (q_hbm, k_hbm, v_hbm)
    bufs = (qb, kb, vb)

    def target(i):
        g = grp ^ (groups - 1 - i // OWNERS)
        p = i % OWNERS
        return g * OWNERS + p, place(g, p)

    def push(t, u, dev):
        src = raw[t].at[:, cols(u // split)]
        slot = me % nq if t == 0 else me
        sem = q_recv.at[slot] if t == 0 else kv_recv.at[t - 1]

        @pl.when(dev != me)
        def _():
            remote(src, bufs[t].at[slot], s_send.at[t, u], sem, dev).start()

        @pl.when(dev == me)
        def _():
            pltpu.make_async_copy(src, bufs[t].at[slot], sem).start()

    def push_kv(i, c):
        u, dev = target(i)
        push(1, u, dev)
        push(2, u, dev)
        return c

    def push_q(i, c):
        u, dev = target(i)

        @pl.when(u % split == me // nq)
        def _():
            push(0, u, dev)

        return c

    lax.fori_loop(0, groups * OWNERS, push_kv, 0)
    lax.fori_loop(0, groups * OWNERS, push_q, 0)
    w_out_copy = pltpu.make_async_copy(w_out_hbm, w_out_v, loc.at[0])
    w_final_copy = pltpu.make_async_copy(w_final_hbm, w_final_v, loc.at[1])
    w_out_copy.start()
    w_final_copy.start()

    def near_order(i, quads):
        z = grp % quads
        outer = (z % 2) == (z // (quads // 2))
        return z ^ jnp.where(outer | (i < 2), i, i ^ 1)

    factor = math.log2(math.e) / math.sqrt(HEAD_DIM)
    keys = n * tok
    chunk = min(keys, CHUNK)
    pair = 2 * tok

    def scores(qh, c):
        kh = kb[pl.ds(c * (chunk // tok), chunk // tok)].reshape(chunk, HEAD_DIM)
        s = lax.dot_general(qh, kh, (((1,), (1,)), ((), ())), preferred_element_type=F32)
        return s * factor

    def weigh(s, top, c):
        vh = vb[pl.ds(c * (chunk // tok), chunk // tok)].reshape(chunk, HEAD_DIM)
        p = jnp.exp2(s - top).astype(BF)
        return mm(p, jnp.concatenate([vh, jnp.ones((chunk, HEAD_DIM), BF)], axis=1))

    def attend(i, carry):
        slot = QUAD * near_order(i // 2, quads) + 2 * (i % 2)
        for e in range(2):
            arrived(qb.at[slot + e], q_recv.at[slot + e])
        qh = qb[pl.ds(slot, 2)].reshape(pair, HEAD_DIM)
        if chunk == keys:
            s = scores(qh, 0)
            acc = weigh(s, jnp.max(s, axis=1, keepdims=True), 0)
        else:

            def step(c, state):
                top, acc = state
                s = scores(qh, c)
                new = jnp.maximum(top, jnp.max(s, axis=1, keepdims=True))
                return new, acc * jnp.exp2(top - new) + weigh(s, new, c)

            first = jnp.full((pair, 1), -1e30, F32), jnp.zeros((pair, 2 * HEAD_DIM), F32)
            acc = lax.fori_loop(0, keys // chunk, step, first)[1]
        ob[pl.ds(slot, 2)] = (acc[:, :HEAD_DIM] / acc[:, HEAD_DIM:]).astype(BF).reshape(2, tok, HEAD_DIM)
        for e in range(2):
            dev = origin + slot + e

            @pl.when(dev != me)
            def _(e=e, dev=dev):
                remote(ob.at[slot + e], att.at[head], o_send.at[slot + e], o_recv.at[head], dev).start()

            @pl.when(dev == me)
            def _(e=e):
                pltpu.make_async_copy(ob.at[slot + e], att.at[head], o_recv.at[head]).start()

        return carry

    @pl.when(mine < OWNERS)
    def _():
        arrived(kb, kv_recv.at[0])
        arrived(vb, kv_recv.at[1])
        lax.fori_loop(0, nq // 2, attend, 0)

    def sent(i, c):
        u, dev = target(i)
        for t in range(3):
            slot = me % nq if t == 0 else me

            @pl.when((dev != me) & ((t > 0) | (u % split == me // nq)))
            def _(t=t, slot=slot):
                remote(raw[t].at[:, cols(u // split)], bufs[t].at[slot], s_send.at[t, u], e_recv.at[0], dev).wait_send()

        return c

    lax.fori_loop(0, groups * OWNERS, sent, 0)
    w_out_copy.wait()
    for i in range(HEADS // OWNERS):
        first = OWNERS * near_order(i, HEADS // OWNERS)
        for e in range(OWNERS):
            arrived(att.at[first + e], o_recv.at[first + e])
        lhs = jnp.concatenate([att[first + e] for e in range(OWNERS)], axis=1)
        rows = pl.ds(pl.multiple_of(first * HEAD_DIM, OWNERS * HEAD_DIM), OWNERS * HEAD_DIM)
        term = mm(lhs, w_out_v[rows])
        proj[...] = term if i == 0 else proj[...] + term
    projected = proj[...]
    centered = projected - jnp.mean(projected, axis=1, keepdims=True)
    variance = jnp.mean(centered * centered, axis=1, keepdims=True)
    normed = (
        centered * lax.rsqrt(variance + 1e-06) * (1.0 + scale_ref[...]) + shift_ref[...]
    ).astype(BF)
    w_final_copy.wait()
    patches = lax.dot_general(
        normed, w_final_v[...], (((1,), (1,)), ((), ())), preferred_element_type=F32
    ).astype(BF)

    ch = iota((4 * LATENT_CH, 128), 0)
    lane = iota((4 * LATENT_CH, 128), 1)
    base = 4 * (lane % 16) + 2 * (lane // 64)
    xcol = (lane // 16) % 4
    row = iota((tok, tok), 0)
    col = iota((tok, tok), 1)
    w = row // rows_dev
    here = (row % rows_dev) * n + w
    picks = (
        ((col == here - 1) & (w > 0), (xcol == 0) & (ch == base + 1)),
        ((col == here) & (w == 0), (xcol == 0) & (ch == base)),
        (col == here, ((xcol == 1) & (ch == base)) | ((xcol == 2) & (ch == base + 1))),
        ((col == here + 1) & (w < n - 1), (xcol == 3) & (ch == base)),
        ((col == here) & (w == n - 1), (xcol == 3) & (ch == base + 1)),
    )
    window = None
    for rows_pick, ch_pick in picks:
        term = mm(ones_where(rows_pick), mm(patches, ones_where(ch_pick)).astype(BF))
        window = term if window is None else window + term
    send_b[...] = window.reshape(n, rows_dev, 128)

    def e_copy(i):
        dev = (me + i) % n
        return remote(send_b.at[dev], recv_b.at[me], e_send.at[i], e_recv.at[i], dev)

    def e_start(i, c):
        e_copy(i).start()
        return c

    def e_wait(i, c):
        src = (me + n - i) % n
        remote(recv_b.at[src], recv_b.at[src], e_send.at[i], e_recv.at[i], src).wait_recv()
        e_copy(i).wait_send()
        return c

    lax.fori_loop(1, n, e_start, 0)
    recv_b[me] = send_b[me]
    lax.fori_loop(1, n, e_wait, 0)

    def returned(slot, c):
        @pl.when(origin + slot != me)
        def _():
            remote(ob.at[slot], att.at[head], o_send.at[slot], e_recv.at[0], origin + slot).wait_send()

        return c

    @pl.when(mine < OWNERS)
    def _():
        lax.fori_loop(0, nq, returned, 0)

    out_ref[...] = recv_b[...].reshape(out_ref.shape)


def conv_kernel(got_ref, conv_v, bias_ref, out_ref, big_w):
    out_ch = conv_v.shape[1]
    big_w[...] = jnp.zeros(big_w.shape, BF)
    for a in range(3):
        for e in range(3):
            for b in range(3):
                for s in range(2):
                    big_w[
                        (a * 3 + e) * 64 + (b + s) * 16 : (a * 3 + e) * 64 + (b + s) * 16 + 16,
                        s * out_ch : (s + 1) * out_ch,
                    ] = conv_v[(9 * a + 3 * b + e) * 16 : (9 * a + 3 * b + e) * 16 + 16, :]
    got = got_ref[...]
    turned = pltpu.roll(got, 64, 1)
    low = iota(got.shape, 1) < 64
    lo = jnp.concatenate([jnp.where(low, got, 0.0), jnp.where(low, turned, 0.0)], axis=0).astype(BF)
    hi = jnp.concatenate([jnp.where(low, 0.0, turned), jnp.where(low, 0.0, got)], axis=0).astype(BF)
    cells = FRAMES * 2 * ROWS
    orow = iota((cells, cells), 0)
    ocol = iota((cells, cells), 1)
    of = orow // (2 * ROWS)
    oy = orow % (2 * ROWS)

    def pick(idx):
        a, e = idx // 3, idx % 3
        sf = jnp.maximum(of + (a - 2), 0)
        sy = jnp.clip(oy + (e - 1), 0, 2 * ROWS - 1)
        return ones_where(ocol == (sy % 2) * (FRAMES * ROWS) + sf * ROWS + sy // 2)

    feats = []
    for pair in range(5):
        x = mm(pick(2 * pair), lo)
        if 2 * pair + 1 < 9:
            x = x + mm(pick(2 * pair + 1), hi)
        feats.append(x.astype(BF))
    feats = jnp.concatenate(feats, axis=1)
    for s in range(2):
        res = mm(feats, big_w[:, s * out_ch : (s + 1) * out_ch]) + bias_ref[...]
        res = res.astype(BF)
        for f in range(FRAMES):
            out_ref[f, s] = res[f * 2 * ROWS : (f + 1) * 2 * ROWS]


def shards(queries, keys, values, w_out, shift_mod, scale_mod, w_final, conv_weight, conv_bias):
    n = lax.axis_size("seq")
    split = n * OWNERS // (QUAD * HEADS)
    tok = queries.shape[0]
    d = w_out.shape[1]
    out_ch = conv_weight.shape[1]
    vm = pl.BlockSpec(memory_space=pltpu.VMEM)
    hbm = pl.BlockSpec(memory_space=pltpu.HBM)
    dma = pltpu.SemaphoreType.DMA
    nq = n // split
    got = pl.pallas_call(
        functools.partial(kernel, n, split),
        out_shape=jax.ShapeDtypeStruct((FRAMES * ROWS, 128), F32),
        in_specs=[hbm, hbm, hbm, hbm, vm, vm, hbm],
        out_specs=vm,
        scratch_shapes=[
            pltpu.VMEM((nq, tok, HEAD_DIM), BF),
            pltpu.VMEM((n, tok, HEAD_DIM), BF),
            pltpu.VMEM((n, tok, HEAD_DIM), BF),
            pltpu.VMEM((nq, tok, HEAD_DIM), BF),
            pltpu.VMEM((HEADS, tok, HEAD_DIM), BF),
            pltpu.VMEM(w_out.shape, BF),
            pltpu.VMEM(w_final.shape[::-1], BF),
            pltpu.VMEM((tok, d), F32),
            pltpu.VMEM((n, tok // n, 128), F32),
            pltpu.VMEM((n, tok // n, 128), F32),
            dma((3, HEADS * split)), dma((2,)), dma((nq,)),
            dma((nq,)), dma((HEADS,)),
            dma((n,)), dma((n,)),
            dma((2,)),
        ],
        compiler_params=pltpu.CompilerParams(
            collective_id=0, has_side_effects=True, vmem_limit_bytes=56 * 1024 * 1024
        ),
        name="fused",
    )(
        queries, keys, values, w_out,
        shift_mod.reshape(1, d), scale_mod.reshape(1, d), w_final.T,
    )
    return pl.pallas_call(
        conv_kernel,
        out_shape=jax.ShapeDtypeStruct((FRAMES, 2, 2 * ROWS, out_ch), BF),
        in_specs=[vm, vm, vm],
        out_specs=vm,
        scratch_shapes=[pltpu.VMEM((640, 2 * out_ch), BF)],
        name="conv",
    )(got, conv_weight, conv_bias.reshape(1, out_ch))


def solution(mesh):
    placed = (
        P(("groups", "seq"), None),
        P(("groups", "seq"), None),
        P(("groups", "seq"), None),
        P(),
        P("groups"),
        P("groups"),
        P(),
        P(),
        P(),
    )
    return jax.shard_map(
        shards,
        mesh=mesh,
        in_specs=placed,
        out_specs=P("groups", "seq", None, None),
        check_vma=False,
    )
```

```python
import functools
import math

import jax
import jax.numpy as jnp
from jax import lax
from jax.experimental import pallas as pl
from jax.experimental.pallas import tpu as pltpu
from jax.sharding import PartitionSpec as P

HEADS = 12
HEAD_DIM = 128
QUAD = 4
OWNERS = 3
CHUNK = 2048
LATENT_CH = 16
FRAMES = 4
ROWS = 32
BF = jnp.bfloat16
F32 = jnp.float32


def mm(a, b):
    return lax.dot_general(a, b, (((1,), (0,)), ((), ())), preferred_element_type=F32)


def iota(shape, dim):
    return lax.broadcasted_iota(jnp.int32, shape, dim)


def ones_where(cond):
    return jnp.where(cond, 1.0, 0.0).astype(BF)


def kernel(
    n, split,
    q_hbm, k_hbm, v_hbm, w_out_hbm, shift_hbm, scale_hbm, w_final_hbm,
    out_ref,
    qb, kb, vb, ob, att, w_out_v, shift_v, scale_v, w_final_v, proj, send_b, recv_b,
    s_send, kv_recv, q_recv, o_send, o_recv, e_send, e_recv, loc,
):
    me = lax.axis_index("seq")
    grp = me // QUAD
    tok = q_hbm.shape[0]
    rows_dev = tok // n
    groups = n // QUAD
    nq = n // split
    quads = nq // QUAD

    def cols(h):
        return pl.ds(pl.multiple_of(h * HEAD_DIM, 128), HEAD_DIM)

    def remote(src, dst, ssem, rsem, dev):
        return pltpu.make_async_remote_copy(
            src_ref=src, dst_ref=dst, send_sem=ssem, recv_sem=rsem,
            device_id={"seq": dev}, device_id_type=pl.DeviceIdType.MESH,
        )

    def arrived(ref, sem):
        pltpu.make_async_copy(ref, ref, sem).wait()

    def place(g, p):
        return g * QUAD + (p + 2 * (g % 2)) % QUAD

    mine = (me % QUAD + QUAD - 2 * (grp % 2)) % QUAD
    unit = grp * OWNERS + mine
    head = unit // split
    origin = (unit % split) * nq

    barrier = pltpu.get_barrier_semaphore()

    def greet(i, c):
        pl.semaphore_signal(
            barrier, inc=1, device_id={"seq": me ^ (n - 1 - i)}, device_id_type=pl.DeviceIdType.MESH
        )
        return c

    lax.fori_loop(0, n - 1, greet, 0)
    pl.semaphore_wait(barrier, n - 1)

    raw = (q_hbm, k_hbm, v_hbm)
    bufs = (qb, kb, vb)

    def target(i):
        g = grp ^ (groups - 1 - i // OWNERS)
        p = i % OWNERS
        return g * OWNERS + p, place(g, p)

    def push(t, u, dev):
        src = raw[t].at[:, cols(u // split)]
        slot = me % nq if t == 0 else me
        sem = q_recv.at[slot] if t == 0 else kv_recv.at[t - 1]

        @pl.when(dev != me)
        def _():
            remote(src, bufs[t].at[slot], s_send.at[t, u], sem, dev).start()

        @pl.when(dev == me)
        def _():
            pltpu.make_async_copy(src, bufs[t].at[slot], sem).start()

    def push_kv(i, c):
        u, dev = target(i)
        push(1, u, dev)
        push(2, u, dev)
        return c

    def push_q(i, c):
        u, dev = target(i)

        @pl.when(u % split == me // nq)
        def _():
            push(0, u, dev)

        return c

    lax.fori_loop(0, groups * OWNERS, push_kv, 0)
    lax.fori_loop(0, groups * OWNERS, push_q, 0)
    loads = [
        pltpu.make_async_copy(src, dst, loc.at[i])
        for i, (src, dst) in enumerate(
            ((w_out_hbm, w_out_v), (shift_hbm, shift_v), (scale_hbm, scale_v), (w_final_hbm, w_final_v))
        )
    ]
    for c in loads:
        c.start()

    def near_order(i, quads):
        z = grp % quads
        outer = (z % 2) == (z // (quads // 2))
        return z ^ jnp.where(outer | (i < 2), i, i ^ 1)

    factor = math.log2(math.e) / math.sqrt(HEAD_DIM)
    keys = n * tok
    chunk = min(keys, CHUNK)
    pair = 2 * tok

    def scores(qh, c):
        kh = kb[pl.ds(c * (chunk // tok), chunk // tok)].reshape(chunk, HEAD_DIM)
        s = lax.dot_general(qh, kh, (((1,), (1,)), ((), ())), preferred_element_type=F32)
        return s * factor

    def weigh(s, top, c):
        vh = vb[pl.ds(c * (chunk // tok), chunk // tok)].reshape(chunk, HEAD_DIM)
        p = jnp.exp2(s - top).astype(BF)
        return mm(p, jnp.concatenate([vh, jnp.ones((chunk, HEAD_DIM), BF)], axis=1))

    def attend(i, carry):
        slot = QUAD * near_order(i // 2, quads) + 2 * (i % 2)
        for e in range(2):
            arrived(qb.at[slot + e], q_recv.at[slot + e])
        qh = qb[pl.ds(slot, 2)].reshape(pair, HEAD_DIM)
        if chunk == keys:
            s = scores(qh, 0)
            acc = weigh(s, jnp.max(s, axis=1, keepdims=True), 0)
        else:

            def step(c, state):
                top, acc = state
                s = scores(qh, c)
                new = jnp.maximum(top, jnp.max(s, axis=1, keepdims=True))
                return new, acc * jnp.exp2(top - new) + weigh(s, new, c)

            first = jnp.full((pair, 1), -1e30, F32), jnp.zeros((pair, 2 * HEAD_DIM), F32)
            acc = lax.fori_loop(0, keys // chunk, step, first)[1]
        ob[pl.ds(slot, 2)] = (acc[:, :HEAD_DIM] / acc[:, HEAD_DIM:]).astype(BF).reshape(2, tok, HEAD_DIM)
        for e in range(2):
            dev = origin + slot + e

            @pl.when(dev != me)
            def _(e=e, dev=dev):
                remote(ob.at[slot + e], att.at[head], o_send.at[slot + e], o_recv.at[head], dev).start()

            @pl.when(dev == me)
            def _(e=e):
                pltpu.make_async_copy(ob.at[slot + e], att.at[head], o_recv.at[head]).start()

        return carry

    @pl.when(mine < OWNERS)
    def _():
        arrived(kb, kv_recv.at[0])
        arrived(vb, kv_recv.at[1])
        lax.fori_loop(0, nq // 2, attend, 0)

    def sent(i, c):
        u, dev = target(i)
        for t in range(3):
            slot = me % nq if t == 0 else me

            @pl.when((dev != me) & ((t > 0) | (u % split == me // nq)))
            def _(t=t, slot=slot):
                remote(raw[t].at[:, cols(u // split)], bufs[t].at[slot], s_send.at[t, u], e_recv.at[0], dev).wait_send()

        return c

    lax.fori_loop(0, groups * OWNERS, sent, 0)
    for c in loads:
        c.wait()
    for i in range(HEADS // OWNERS):
        first = OWNERS * near_order(i, HEADS // OWNERS)
        for e in range(OWNERS):
            arrived(att.at[first + e], o_recv.at[first + e])
        lhs = jnp.concatenate([att[first + e] for e in range(OWNERS)], axis=1)
        rows = pl.ds(pl.multiple_of(first * HEAD_DIM, OWNERS * HEAD_DIM), OWNERS * HEAD_DIM)
        term = mm(lhs, w_out_v[rows])
        proj[...] = term if i == 0 else proj[...] + term
    projected = proj[...]
    centered = projected - jnp.mean(projected, axis=1, keepdims=True)
    variance = jnp.mean(centered * centered, axis=1, keepdims=True)
    normed = (
        centered * lax.rsqrt(variance + 1e-06) * (1.0 + scale_v[...]) + shift_v[...]
    ).astype(BF)
    patches = lax.dot_general(
        normed, w_final_v[...], (((1,), (1,)), ((), ())), preferred_element_type=F32
    ).astype(BF)

    ch = iota((4 * LATENT_CH, 128), 0)
    lane = iota((4 * LATENT_CH, 128), 1)
    base = 4 * (lane % 16) + 2 * (lane // 64)
    xcol = (lane // 16) % 4
    row = iota((tok, tok), 0)
    col = iota((tok, tok), 1)
    w = row // rows_dev
    here = (row % rows_dev) * n + w
    picks = (
        ((col == here - 1) & (w > 0), (xcol == 0) & (ch == base + 1)),
        ((col == here) & (w == 0), (xcol == 0) & (ch == base)),
        (col == here, ((xcol == 1) & (ch == base)) | ((xcol == 2) & (ch == base + 1))),
        ((col == here + 1) & (w < n - 1), (xcol == 3) & (ch == base)),
        ((col == here) & (w == n - 1), (xcol == 3) & (ch == base + 1)),
    )
    window = None
    for rows_pick, ch_pick in picks:
        term = mm(ones_where(rows_pick), mm(patches, ones_where(ch_pick)).astype(BF))
        window = term if window is None else window + term
    send_b[...] = window.reshape(n, rows_dev, 128)

    def e_copy(i):
        dev = (me + i) % n
        return remote(send_b.at[dev], recv_b.at[me], e_send.at[i], e_recv.at[i], dev)

    def e_start(i, c):
        e_copy(i).start()
        return c

    def e_wait(i, c):
        src = (me + n - i) % n
        remote(recv_b.at[src], recv_b.at[src], e_send.at[i], e_recv.at[i], src).wait_recv()
        e_copy(i).wait_send()
        return c

    lax.fori_loop(1, n, e_start, 0)
    recv_b[me] = send_b[me]
    lax.fori_loop(1, n, e_wait, 0)

    def returned(slot, c):
        @pl.when(origin + slot != me)
        def _():
            remote(ob.at[slot], att.at[head], o_send.at[slot], e_recv.at[0], origin + slot).wait_send()

        return c

    @pl.when(mine < OWNERS)
    def _():
        lax.fori_loop(0, nq, returned, 0)

    out_ref[...] = recv_b[...].reshape(out_ref.shape)


def conv_kernel(got_ref, conv_v, bias_ref, out_ref, big_w):
    out_ch = conv_v.shape[1]
    big_w[...] = jnp.zeros(big_w.shape, BF)
    for a in range(3):
        for e in range(3):
            for b in range(3):
                for s in range(2):
                    big_w[
                        (a * 3 + e) * 64 + (b + s) * 16 : (a * 3 + e) * 64 + (b + s) * 16 + 16,
                        s * out_ch : (s + 1) * out_ch,
                    ] = conv_v[(9 * a + 3 * b + e) * 16 : (9 * a + 3 * b + e) * 16 + 16, :]
    got = got_ref[...]
    turned = pltpu.roll(got, 64, 1)
    low = iota(got.shape, 1) < 64
    lo = jnp.concatenate([jnp.where(low, got, 0.0), jnp.where(low, turned, 0.0)], axis=0).astype(BF)
    hi = jnp.concatenate([jnp.where(low, 0.0, turned), jnp.where(low, 0.0, got)], axis=0).astype(BF)
    cells = FRAMES * 2 * ROWS
    orow = iota((cells, cells), 0)
    ocol = iota((cells, cells), 1)
    of = orow // (2 * ROWS)
    oy = orow % (2 * ROWS)

    def pick(idx):
        a, e = idx // 3, idx % 3
        sf = jnp.maximum(of + (a - 2), 0)
        sy = jnp.clip(oy + (e - 1), 0, 2 * ROWS - 1)
        return ones_where(ocol == (sy % 2) * (FRAMES * ROWS) + sf * ROWS + sy // 2)

    feats = []
    for pair in range(5):
        x = mm(pick(2 * pair), lo)
        if 2 * pair + 1 < 9:
            x = x + mm(pick(2 * pair + 1), hi)
        feats.append(x.astype(BF))
    feats = jnp.concatenate(feats, axis=1)
    for s in range(2):
        res = mm(feats, big_w[:, s * out_ch : (s + 1) * out_ch]) + bias_ref[...]
        res = res.astype(BF)
        for f in range(FRAMES):
            out_ref[f, s] = res[f * 2 * ROWS : (f + 1) * 2 * ROWS]


def shards(queries, keys, values, w_out, shift_mod, scale_mod, w_final, conv_weight, conv_bias):
    n = lax.axis_size("seq")
    split = n * OWNERS // (QUAD * HEADS)
    tok = queries.shape[0]
    d = w_out.shape[1]
    out_ch = conv_weight.shape[1]
    vm = pl.BlockSpec(memory_space=pltpu.VMEM)
    hbm = pl.BlockSpec(memory_space=pltpu.HBM)
    dma = pltpu.SemaphoreType.DMA
    nq = n // split
    got = pl.pallas_call(
        functools.partial(kernel, n, split),
        out_shape=jax.ShapeDtypeStruct((FRAMES * ROWS, 128), F32),
        in_specs=[hbm] * 7,
        out_specs=vm,
        scratch_shapes=[
            pltpu.VMEM((nq, tok, HEAD_DIM), BF),
            pltpu.VMEM((n, tok, HEAD_DIM), BF),
            pltpu.VMEM((n, tok, HEAD_DIM), BF),
            pltpu.VMEM((nq, tok, HEAD_DIM), BF),
            pltpu.VMEM((HEADS, tok, HEAD_DIM), BF),
            pltpu.VMEM(w_out.shape, BF),
            pltpu.VMEM((1, d), F32),
            pltpu.VMEM((1, d), F32),
            pltpu.VMEM(w_final.shape[::-1], BF),
            pltpu.VMEM((tok, d), F32),
            pltpu.VMEM((n, tok // n, 128), F32),
            pltpu.VMEM((n, tok // n, 128), F32),
            dma((3, HEADS * split)), dma((2,)), dma((nq,)),
            dma((nq,)), dma((HEADS,)),
            dma((n,)), dma((n,)),
            dma((4,)),
        ],
        compiler_params=pltpu.CompilerParams(
            collective_id=0, has_side_effects=True, vmem_limit_bytes=32 * 1024 * 1024
        ),
        name="fused",
    )(
        *(
            pltpu.with_memory_space_constraint(x, pltpu.HBM)
            for x in (
                queries, keys, values, w_out,
                shift_mod.reshape(1, d), scale_mod.reshape(1, d), w_final.T,
            )
        )
    )
    return pl.pallas_call(
        conv_kernel,
        out_shape=jax.ShapeDtypeStruct((FRAMES, 2, 2 * ROWS, out_ch), BF),
        in_specs=[vm, vm, vm],
        out_specs=vm,
        scratch_shapes=[pltpu.VMEM((640, 2 * out_ch), BF)],
        compiler_params=pltpu.CompilerParams(vmem_limit_bytes=8 * 1024 * 1024),
        name="conv",
    )(got, conv_weight, conv_bias.reshape(1, out_ch))


def solution(mesh):
    placed = (
        P(("groups", "seq"), None),
        P(("groups", "seq"), None),
        P(("groups", "seq"), None),
        P(),
        P("groups"),
        P("groups"),
        P(),
        P(),
        P(),
    )
    return jax.shard_map(
        shards,
        mesh=mesh,
        in_specs=placed,
        out_specs=P("groups", "seq", None, None),
        check_vma=False,
    )
```

```python
import functools
import math

import jax
import jax.numpy as jnp
from jax import lax
from jax.experimental import pallas as pl
from jax.experimental.pallas import tpu as pltpu
from jax.sharding import PartitionSpec as P

HEADS = 12
HEAD_DIM = 128
QUAD = 4
OWNERS = 3
CHUNK = 2048
LATENT_CH = 16
FRAMES = 4
ROWS = 32
BF = jnp.bfloat16
F32 = jnp.float32


def mm(a, b):
    return lax.dot_general(a, b, (((1,), (0,)), ((), ())), preferred_element_type=F32)


def iota(shape, dim):
    return lax.broadcasted_iota(jnp.int32, shape, dim)


def ones_where(cond):
    return jnp.where(cond, 1.0, 0.0).astype(BF)


def kernel(
    n, split,
    q_hbm, k_hbm, v_hbm, w_out_hbm, shift_hbm, scale_hbm, w_final_hbm,
    out_ref,
    qb, kb, vb, ob, att, w_out_v, shift_v, scale_v, w_final_v, proj, send_b, recv_b,
    s_send, kv_recv, q_recv, o_recv, e_recv, loc,
):
    me = lax.axis_index("seq")
    grp = me // QUAD
    tok = q_hbm.shape[0]
    rows_dev = tok // n
    groups = n // QUAD
    nq = n // split
    quads = nq // QUAD

    def cols(h):
        return pl.ds(pl.multiple_of(h * HEAD_DIM, 128), HEAD_DIM)

    def remote(src, dst, ssem, rsem, dev):
        return pltpu.make_async_remote_copy(
            src_ref=src, dst_ref=dst, send_sem=ssem, recv_sem=rsem,
            device_id={"seq": dev}, device_id_type=pl.DeviceIdType.MESH,
        )

    def arrived(ref, sem):
        pltpu.make_async_copy(ref, ref, sem).wait()

    def place(g, p):
        return g * QUAD + (p + 2 * (g % 2)) % QUAD

    mine = (me % QUAD + QUAD - 2 * (grp % 2)) % QUAD
    unit = grp * OWNERS + mine
    head = unit // split
    origin = (unit % split) * nq

    barrier = pltpu.get_barrier_semaphore()

    def greet(i, c):
        pl.semaphore_signal(
            barrier, inc=1, device_id={"seq": me ^ (n - 1 - i)}, device_id_type=pl.DeviceIdType.MESH
        )
        return c

    lax.fori_loop(0, n - 1, greet, 0)
    pl.semaphore_wait(barrier, n - 1)

    raw = (q_hbm, k_hbm, v_hbm)
    bufs = (qb, kb, vb)

    def target(i):
        g = grp ^ (groups - 1 - i // OWNERS)
        p = i % OWNERS
        return g * OWNERS + p, place(g, p)

    def push(t, u, dev):
        src = raw[t].at[:, cols(u // split)]
        slot = me % nq if t == 0 else me
        sem = q_recv.at[slot] if t == 0 else kv_recv.at[t - 1]

        @pl.when(dev != me)
        def _():
            remote(src, bufs[t].at[slot], s_send.at[0], sem, dev).start()

        @pl.when(dev == me)
        def _():
            pltpu.make_async_copy(src, bufs[t].at[slot], sem).start()

    def push_kv(i, c):
        u, dev = target(i)
        push(1, u, dev)
        push(2, u, dev)
        return c

    def push_q(i, c):
        u, dev = target(i)

        @pl.when(u % split == me // nq)
        def _():
            push(0, u, dev)

        return c

    lax.fori_loop(0, groups * OWNERS, push_kv, 0)
    lax.fori_loop(0, groups * OWNERS, push_q, 0)
    loads = [
        pltpu.make_async_copy(src, dst, loc.at[i])
        for i, (src, dst) in enumerate(
            ((w_out_hbm, w_out_v), (shift_hbm, shift_v), (scale_hbm, scale_v), (w_final_hbm, w_final_v))
        )
    ]
    for c in loads:
        c.start()

    def near_order(i, quads):
        z = grp % quads
        outer = (z % 2) == (z // (quads // 2))
        return z ^ jnp.where(outer & (i > 1), i ^ 1, i)

    factor = math.log2(math.e) / math.sqrt(HEAD_DIM)
    keys = n * tok
    chunk = min(keys, CHUNK)
    pair = 2 * tok

    def scores(qh, c):
        kh = kb[pl.ds(c * (chunk // tok), chunk // tok)].reshape(chunk, HEAD_DIM)
        s = lax.dot_general(qh, kh, (((1,), (1,)), ((), ())), preferred_element_type=F32)
        return s * factor

    def weigh(s, top, c):
        vh = vb[pl.ds(c * (chunk // tok), chunk // tok)].reshape(chunk, HEAD_DIM)
        p = jnp.exp2(s - top).astype(BF)
        return mm(p, jnp.concatenate([vh, jnp.ones((chunk, HEAD_DIM), BF)], axis=1))

    def attend(i, carry):
        slot = QUAD * near_order(i // 2, quads) + 2 * (i % 2)
        for e in range(2):
            arrived(qb.at[slot + e], q_recv.at[slot + e])
        qh = qb[pl.ds(slot, 2)].reshape(pair, HEAD_DIM)
        if chunk == keys:
            s = scores(qh, 0)
            acc = weigh(s, jnp.max(s, axis=1, keepdims=True), 0)
        else:

            def step(c, state):
                top, acc = state
                s = scores(qh, c)
                new = jnp.maximum(top, jnp.max(s, axis=1, keepdims=True))
                return new, acc * jnp.exp2(top - new) + weigh(s, new, c)

            first = jnp.full((pair, 1), -1e30, F32), jnp.zeros((pair, 2 * HEAD_DIM), F32)
            acc = lax.fori_loop(0, keys // chunk, step, first)[1]
        ob[pl.ds(slot, 2)] = (acc[:, :HEAD_DIM] / acc[:, HEAD_DIM:]).astype(BF).reshape(2, tok, HEAD_DIM)
        for e in range(2):
            dev = origin + slot + e

            @pl.when(dev != me)
            def _(e=e, dev=dev):
                remote(ob.at[slot + e], att.at[head], s_send.at[1], o_recv.at[head], dev).start()

            @pl.when(dev == me)
            def _(e=e):
                pltpu.make_async_copy(ob.at[slot + e], att.at[head], o_recv.at[head]).start()

        return carry

    @pl.when(mine < OWNERS)
    def _():
        arrived(kb, kv_recv.at[0])
        arrived(vb, kv_recv.at[1])
        lax.fori_loop(0, nq // 2, attend, 0)

    for c in loads:
        c.wait()
    for i in range(HEADS // OWNERS):
        first = OWNERS * near_order(i, HEADS // OWNERS)
        for e in range(OWNERS):
            arrived(att.at[first + e], o_recv.at[first + e])
        lhs = jnp.concatenate([att[first + e] for e in range(OWNERS)], axis=1)
        rows = pl.ds(pl.multiple_of(first * HEAD_DIM, OWNERS * HEAD_DIM), OWNERS * HEAD_DIM)
        term = mm(lhs, w_out_v[rows])
        proj[...] = term if i == 0 else proj[...] + term
    projected = proj[...]
    centered = projected - jnp.mean(projected, axis=1, keepdims=True)
    variance = jnp.mean(centered * centered, axis=1, keepdims=True)
    normed = (
        centered * lax.rsqrt(variance + 1e-06) * (1.0 + scale_v[...]) + shift_v[...]
    ).astype(BF)
    patches = lax.dot_general(
        normed, w_final_v[...], (((1,), (1,)), ((), ())), preferred_element_type=F32
    ).astype(BF)

    ch = iota((4 * LATENT_CH, 128), 0)
    lane = iota((4 * LATENT_CH, 128), 1)
    base = 4 * (lane % 16) + 2 * (lane // 64)
    xcol = (lane // 16) % 4
    row = iota((tok, tok), 0)
    col = iota((tok, tok), 1)
    w = row // rows_dev
    here = (row % rows_dev) * n + w
    picks = (
        ((col == here - 1) & (w > 0), (xcol == 0) & (ch == base + 1)),
        ((col == here) & (w == 0), (xcol == 0) & (ch == base)),
        (col == here, ((xcol == 1) & (ch == base)) | ((xcol == 2) & (ch == base + 1))),
        ((col == here + 1) & (w < n - 1), (xcol == 3) & (ch == base)),
        ((col == here) & (w == n - 1), (xcol == 3) & (ch == base + 1)),
    )
    window = None
    for rows_pick, ch_pick in picks:
        term = mm(ones_where(rows_pick), mm(patches, ones_where(ch_pick)).astype(BF))
        window = term if window is None else window + term
    send_b[...] = window.reshape(n, rows_dev, 128)

    def exchange(i, c):
        dev = me ^ (n - 1 - i)
        remote(send_b.at[dev], recv_b.at[me], s_send.at[2], e_recv.at[0], dev).start()
        return c

    lax.fori_loop(0, n - 1, exchange, 0)
    recv_b[me] = send_b[me]
    owner = mine < OWNERS
    units = groups * OWNERS
    gone = (
        (units - 1, 0, ~owner),
        (units - 1, 0, ~owner),
        (HEADS - 1, 0, ~(owner & (unit % split == me // nq))),
    )
    for count, sem, one_more in gone:
        arrived(kb.at[pl.ds(0, count)], s_send.at[sem])

        @pl.when(one_more)
        def _(sem=sem):
            arrived(kb.at[0], s_send.at[sem])

    @pl.when(owner)
    def _():
        arrived(ob.at[pl.ds(0, nq - 1)], s_send.at[1])

        @pl.when(origin // nq != me // nq)
        def _():
            arrived(ob.at[0], s_send.at[1])

    arrived(recv_b.at[pl.ds(0, n - 1)], e_recv.at[0])
    arrived(send_b.at[pl.ds(0, n - 1)], s_send.at[2])
    out_ref[...] = recv_b[...].reshape(out_ref.shape)


def conv_kernel(got_ref, conv_v, bias_ref, out_ref, big_w):
    out_ch = conv_v.shape[1]
    big_w[...] = jnp.zeros(big_w.shape, BF)
    for a in range(3):
        for e in range(3):
            for b in range(3):
                for s in range(2):
                    big_w[
                        (a * 3 + e) * 64 + (b + s) * 16 : (a * 3 + e) * 64 + (b + s) * 16 + 16,
                        s * out_ch : (s + 1) * out_ch,
                    ] = conv_v[(9 * a + 3 * b + e) * 16 : (9 * a + 3 * b + e) * 16 + 16, :]
    got = got_ref[...]
    turned = pltpu.roll(got, 64, 1)
    low = iota(got.shape, 1) < 64
    lo = jnp.concatenate([jnp.where(low, got, 0.0), jnp.where(low, turned, 0.0)], axis=0).astype(BF)
    hi = jnp.concatenate([jnp.where(low, 0.0, turned), jnp.where(low, 0.0, got)], axis=0).astype(BF)
    cells = FRAMES * 2 * ROWS
    orow = iota((cells, cells), 0)
    ocol = iota((cells, cells), 1)
    of = orow // (2 * ROWS)
    oy = orow % (2 * ROWS)

    def pick(idx):
        a, e = idx // 3, idx % 3
        sf = jnp.maximum(of + (a - 2), 0)
        sy = jnp.clip(oy + (e - 1), 0, 2 * ROWS - 1)
        return ones_where(ocol == (sy % 2) * (FRAMES * ROWS) + sf * ROWS + sy // 2)

    feats = []
    for pair in range(5):
        x = mm(pick(2 * pair), lo)
        if 2 * pair + 1 < 9:
            x = x + mm(pick(2 * pair + 1), hi)
        feats.append(x.astype(BF))
    feats = jnp.concatenate(feats, axis=1)
    for s in range(2):
        res = mm(feats, big_w[:, s * out_ch : (s + 1) * out_ch]) + bias_ref[...]
        res = res.astype(BF)
        for f in range(FRAMES):
            out_ref[f, s] = res[f * 2 * ROWS : (f + 1) * 2 * ROWS]


def shards(queries, keys, values, w_out, shift_mod, scale_mod, w_final, conv_weight, conv_bias):
    n = lax.axis_size("seq")
    split = n * OWNERS // (QUAD * HEADS)
    tok = queries.shape[0]
    d = w_out.shape[1]
    out_ch = conv_weight.shape[1]
    vm = pl.BlockSpec(memory_space=pltpu.VMEM)
    hbm = pl.BlockSpec(memory_space=pltpu.HBM)
    dma = pltpu.SemaphoreType.DMA
    nq = n // split
    got = pl.pallas_call(
        functools.partial(kernel, n, split),
        out_shape=jax.ShapeDtypeStruct((FRAMES * ROWS, 128), F32),
        in_specs=[hbm] * 7,
        out_specs=vm,
        scratch_shapes=[
            pltpu.VMEM((nq, tok, HEAD_DIM), BF),
            pltpu.VMEM((n, tok, HEAD_DIM), BF),
            pltpu.VMEM((n, tok, HEAD_DIM), BF),
            pltpu.VMEM((nq, tok, HEAD_DIM), BF),
            pltpu.VMEM((HEADS, tok, HEAD_DIM), BF),
            pltpu.VMEM(w_out.shape, BF),
            pltpu.VMEM((1, d), F32),
            pltpu.VMEM((1, d), F32),
            pltpu.VMEM(w_final.shape[::-1], BF),
            pltpu.VMEM((tok, d), F32),
            pltpu.VMEM((n, tok // n, 128), F32),
            pltpu.VMEM((n, tok // n, 128), F32),
            dma((3,)), dma((2,)), dma((nq,)), dma((HEADS,)), dma((1,)), dma((4,)),
        ],
        compiler_params=pltpu.CompilerParams(
            collective_id=0, has_side_effects=True, vmem_limit_bytes=32 * 1024 * 1024
        ),
        name="fused",
    )(
        *(
            pltpu.with_memory_space_constraint(x, pltpu.HBM)
            for x in (
                queries, keys, values, w_out,
                shift_mod.reshape(1, d), scale_mod.reshape(1, d), w_final.T,
            )
        )
    )
    return pl.pallas_call(
        conv_kernel,
        out_shape=jax.ShapeDtypeStruct((FRAMES, 2, 2 * ROWS, out_ch), BF),
        in_specs=[vm, vm, vm],
        out_specs=vm,
        scratch_shapes=[pltpu.VMEM((640, 2 * out_ch), BF)],
        compiler_params=pltpu.CompilerParams(vmem_limit_bytes=8 * 1024 * 1024),
        name="conv",
    )(got, conv_weight, conv_bias.reshape(1, out_ch))


def solution(mesh):
    placed = (
        P(("groups", "seq"), None),
        P(("groups", "seq"), None),
        P(("groups", "seq"), None),
        P(),
        P("groups"),
        P("groups"),
        P(),
        P(),
        P(),
    )
    return jax.shard_map(
        shards,
        mesh=mesh,
        in_specs=placed,
        out_specs=P("groups", "seq", None, None),
        check_vma=False,
    )
```

```python
import functools
import math

import jax
import jax.numpy as jnp
from jax import lax
from jax.experimental import pallas as pl
from jax.experimental.pallas import tpu as pltpu
from jax.sharding import PartitionSpec as P

HEADS = 12
HEAD_DIM = 128
QUAD = 4
OWNERS = 3
CHUNK = 2048
PICKS = 5
LATENT_CH = 16
FRAMES = 4
ROWS = 32
BF = jnp.bfloat16
F32 = jnp.float32


def mm(a, b):
    return lax.dot_general(a, b, (((1,), (0,)), ((), ())), preferred_element_type=F32)


def iota(shape, dim):
    return lax.broadcasted_iota(jnp.int32, shape, dim)


def ones_where(cond):
    return jnp.where(cond, 1.0, 0.0).astype(BF)


def kernel(
    n, split,
    q_hbm, k_hbm, v_hbm, w_out_hbm, shift_hbm, scale_hbm, w_final_hbm, conv_hbm,
    out_ref, big_w,
    qb, kb, vb, ob, att, w_out_v, shift_v, scale_v, w_final_v, conv_v, row_picks, ch_picks, proj, send_b, recv_b,
    s_send, kv_recv, q_recv, o_recv, e_recv, loc,
):
    me = lax.axis_index("seq")
    grp = me // QUAD
    tok = q_hbm.shape[0]
    rows_dev = tok // n
    groups = n // QUAD
    nq = n // split
    quads = nq // QUAD

    def cols(h):
        return pl.ds(pl.multiple_of(h * HEAD_DIM, 128), HEAD_DIM)

    def remote(src, dst, ssem, rsem, dev):
        return pltpu.make_async_remote_copy(
            src_ref=src, dst_ref=dst, send_sem=ssem, recv_sem=rsem,
            device_id={"seq": dev}, device_id_type=pl.DeviceIdType.MESH,
        )

    def arrived(ref, sem):
        pltpu.make_async_copy(ref, ref, sem).wait()

    def place(g, p):
        return g * QUAD + (p + 2 * (g % 2)) % QUAD

    mine = (me % QUAD + QUAD - 2 * (grp % 2)) % QUAD
    unit = grp * OWNERS + mine
    head = unit // split
    origin = (unit % split) * nq

    barrier = pltpu.get_barrier_semaphore()

    def greet(i, c):
        pl.semaphore_signal(
            barrier, inc=1, device_id={"seq": me ^ (n - 1 - i)}, device_id_type=pl.DeviceIdType.MESH
        )
        return c

    lax.fori_loop(0, n - 1, greet, 0)
    pl.semaphore_wait(barrier, n - 1)

    raw = (q_hbm, k_hbm, v_hbm)
    bufs = (qb, kb, vb)

    def target(i):
        g = grp ^ (groups - 1 - i // OWNERS)
        p = i % OWNERS
        return g * OWNERS + p, place(g, p)

    def push(t, u, dev):
        src = raw[t].at[:, cols(u // split)]
        slot = me % nq if t == 0 else me
        sem = q_recv.at[slot] if t == 0 else kv_recv.at[t - 1]

        @pl.when(dev != me)
        def _():
            remote(src, bufs[t].at[slot], s_send.at[0], sem, dev).start()

        @pl.when(dev == me)
        def _():
            pltpu.make_async_copy(src, bufs[t].at[slot], sem).start()

    def push_kv(i, c):
        u, dev = target(i)
        push(1, u, dev)
        push(2, u, dev)
        return c

    def push_q(i, c):
        u, dev = target(i)

        @pl.when(u % split == me // nq)
        def _():
            push(0, u, dev)

        return c

    lax.fori_loop(0, groups * OWNERS, push_kv, 0)
    lax.fori_loop(0, groups * OWNERS, push_q, 0)
    loads = [
        pltpu.make_async_copy(src, dst, loc.at[i])
        for i, (src, dst) in enumerate(
            ((w_out_hbm, w_out_v), (shift_hbm, shift_v), (scale_hbm, scale_v), (w_final_hbm, w_final_v), (conv_hbm, conv_v))
        )
    ]
    for c in loads[::-1]:
        c.start()

    ch = iota((4 * LATENT_CH, 128), 0)
    lane = iota((4 * LATENT_CH, 128), 1)
    base = 4 * (lane % 16) + 2 * (lane // 64)
    xcol = (lane // 16) % 4
    row = iota((tok, tok), 0)
    col = iota((tok, tok), 1)
    w = row // rows_dev
    here = (row % rows_dev) * n + w
    picks = (
        ((col == here - 1) & (w > 0), (xcol == 0) & (ch == base + 1)),
        ((col == here) & (w == 0), (xcol == 0) & (ch == base)),
        (col == here, ((xcol == 1) & (ch == base)) | ((xcol == 2) & (ch == base + 1))),
        ((col == here + 1) & (w < n - 1), (xcol == 3) & (ch == base)),
        ((col == here) & (w == n - 1), (xcol == 3) & (ch == base + 1)),
    )
    for i, (rows_pick, ch_pick) in enumerate(picks):
        row_picks[:, i * tok : (i + 1) * tok] = ones_where(rows_pick)
        ch_picks[:, i * 128 : (i + 1) * 128] = ones_where(ch_pick)
    loads[-1].wait()
    spread_weights(conv_v, big_w)

    def near_order(i, quads):
        z = grp % quads
        outer = (z % 2) == (z // (quads // 2))
        return z ^ jnp.where(outer & (i > 1), i ^ 1, i)

    factor = math.log2(math.e) / math.sqrt(HEAD_DIM)
    keys = n * tok
    chunk = min(keys, CHUNK)
    pair = 2 * tok

    def scores(qh, c):
        kh = kb[pl.ds(c * (chunk // tok), chunk // tok)].reshape(chunk, HEAD_DIM)
        s = lax.dot_general(qh, kh, (((1,), (1,)), ((), ())), preferred_element_type=F32)
        return s * factor

    def weigh(s, top, c):
        vh = vb[pl.ds(c * (chunk // tok), chunk // tok)].reshape(chunk, HEAD_DIM)
        p = jnp.exp2(s - top).astype(BF)
        return mm(p, jnp.concatenate([vh, jnp.ones((chunk, HEAD_DIM), BF)], axis=1))

    def attend(i, carry):
        slot = QUAD * near_order(i // 2, quads) + 2 * (i % 2)
        for e in range(2):
            arrived(qb.at[slot + e], q_recv.at[slot + e])
        qh = qb[pl.ds(slot, 2)].reshape(pair, HEAD_DIM)
        if chunk == keys:
            s = scores(qh, 0)
            acc = weigh(s, jnp.max(s, axis=1, keepdims=True), 0)
        else:

            def step(c, state):
                top, acc = state
                s = scores(qh, c)
                new = jnp.maximum(top, jnp.max(s, axis=1, keepdims=True))
                return new, acc * jnp.exp2(top - new) + weigh(s, new, c)

            first = jnp.full((pair, 1), -1e30, F32), jnp.zeros((pair, 2 * HEAD_DIM), F32)
            acc = lax.fori_loop(0, keys // chunk, step, first)[1]
        ob[pl.ds(slot, 2)] = (acc[:, :HEAD_DIM] / acc[:, HEAD_DIM:]).astype(BF).reshape(2, tok, HEAD_DIM)
        for e in range(2):
            dev = origin + slot + e

            @pl.when(dev != me)
            def _(e=e, dev=dev):
                remote(ob.at[slot + e], att.at[head], s_send.at[1], o_recv.at[head], dev).start()

            @pl.when(dev == me)
            def _(e=e):
                pltpu.make_async_copy(ob.at[slot + e], att.at[head], o_recv.at[head]).start()

        return carry

    @pl.when(mine < OWNERS)
    def _():
        arrived(kb, kv_recv.at[0])
        arrived(vb, kv_recv.at[1])
        lax.fori_loop(0, nq // 2, attend, 0)

    for c in loads[:-1]:
        c.wait()
    for i in range(HEADS // OWNERS):
        first = OWNERS * near_order(i, HEADS // OWNERS)
        for e in range(OWNERS):
            arrived(att.at[first + e], o_recv.at[first + e])
        lhs = jnp.concatenate([att[first + e] for e in range(OWNERS)], axis=1)
        rows = pl.ds(pl.multiple_of(first * HEAD_DIM, OWNERS * HEAD_DIM), OWNERS * HEAD_DIM)
        term = mm(lhs, w_out_v[rows])
        proj[...] = term if i == 0 else proj[...] + term
    projected = proj[...]
    centered = projected - jnp.mean(projected, axis=1, keepdims=True)
    variance = jnp.mean(centered * centered, axis=1, keepdims=True)
    normed = (
        centered * lax.rsqrt(variance + 1e-06) * (1.0 + scale_v[...]) + shift_v[...]
    ).astype(BF)
    patches = lax.dot_general(
        normed, w_final_v[...], (((1,), (1,)), ((), ())), preferred_element_type=F32
    ).astype(BF)

    spread = mm(patches, ch_picks[...]).astype(BF)
    window = mm(
        row_picks[...], jnp.concatenate([spread[:, i * 128 : (i + 1) * 128] for i in range(PICKS)], axis=0)
    )
    send_b[...] = window.reshape(n, rows_dev, 128)

    def exchange(i, c):
        dev = me ^ (n - 1 - i)
        remote(send_b.at[dev], recv_b.at[me], s_send.at[2], e_recv.at[0], dev).start()
        return c

    lax.fori_loop(0, n - 1, exchange, 0)
    recv_b[me] = send_b[me]
    owner = mine < OWNERS
    units = groups * OWNERS
    gone = (
        (units - 1, 0, ~owner),
        (units - 1, 0, ~owner),
        (HEADS - 1, 0, ~(owner & (unit % split == me // nq))),
    )
    for count, sem, one_more in gone:
        arrived(kb.at[pl.ds(0, count)], s_send.at[sem])

        @pl.when(one_more)
        def _(sem=sem):
            arrived(kb.at[0], s_send.at[sem])

    @pl.when(owner)
    def _():
        arrived(ob.at[pl.ds(0, nq - 1)], s_send.at[1])

        @pl.when(origin // nq != me // nq)
        def _():
            arrived(ob.at[0], s_send.at[1])

    arrived(recv_b.at[pl.ds(0, n - 1)], e_recv.at[0])
    arrived(send_b.at[pl.ds(0, n - 1)], s_send.at[2])
    out_ref[...] = recv_b[...].reshape(out_ref.shape)


def spread_weights(conv_v, big_w):
    out_ch = conv_v.shape[1]
    big_w[...] = jnp.zeros(big_w.shape, BF)
    for a in range(3):
        for e in range(3):
            for b in range(3):
                for s in range(2):
                    row = a * 256 + e * 64 + (b + s) * 16
                    tap = (9 * a + 3 * b + e) * 16
                    big_w[row : row + 16, s * out_ch : (s + 1) * out_ch] = conv_v[tap : tap + 16, :]


def conv_kernel(got_ref, big_w, bias_ref, out_ref, left, right):
    out_ch = bias_ref.shape[1]
    cells = FRAMES * ROWS
    got = got_ref[...]
    turned = pltpu.roll(got, 64, 1)
    low = iota(got.shape, 1) < 64
    row = iota(got.shape, 0) % ROWS
    above = jnp.where(row == 0, got, pltpu.roll(turned, 1, 0))
    below = jnp.where(row == ROWS - 1, turned, pltpu.roll(got, cells - 1, 0))
    left[pl.ds(0, cells, 2), :] = jnp.where(low, above, turned)
    right[pl.ds(0, cells, 2), :] = jnp.where(low, turned, 0.0)
    left[pl.ds(1, cells, 2), :] = got
    right[pl.ds(1, cells, 2), :] = jnp.where(low, below, 0.0)
    taps = jnp.concatenate([left[...], right[...]], axis=1).astype(BF)
    frames = [taps[f * 2 * ROWS : (f + 1) * 2 * ROWS] for f in range(FRAMES)]
    feats = jnp.concatenate(
        [jnp.concatenate([frames[max(f + a - 2, 0)] for f in range(FRAMES)], axis=0) for a in range(3)], axis=1
    )
    for s in range(2):
        res = mm(feats, big_w[:, s * out_ch : (s + 1) * out_ch]) + bias_ref[...]
        res = res.astype(BF)
        for f in range(FRAMES):
            out_ref[f, s] = res[f * 2 * ROWS : (f + 1) * 2 * ROWS]


def shards(queries, keys, values, w_out, shift_mod, scale_mod, w_final, conv_weight, conv_bias):
    n = lax.axis_size("seq")
    split = n * OWNERS // (QUAD * HEADS)
    tok = queries.shape[0]
    d = w_out.shape[1]
    out_ch = conv_weight.shape[1]
    vm = pl.BlockSpec(memory_space=pltpu.VMEM)
    hbm = pl.BlockSpec(memory_space=pltpu.HBM)
    dma = pltpu.SemaphoreType.DMA
    nq = n // split
    got, big_w = pl.pallas_call(
        functools.partial(kernel, n, split),
        out_shape=(
            jax.ShapeDtypeStruct((FRAMES * ROWS, 128), F32),
            jax.ShapeDtypeStruct((768, 2 * out_ch), BF),
        ),
        in_specs=[hbm] * 8,
        out_specs=(vm, vm),
        scratch_shapes=[
            pltpu.VMEM((nq, tok, HEAD_DIM), BF),
            pltpu.VMEM((n, tok, HEAD_DIM), BF),
            pltpu.VMEM((n, tok, HEAD_DIM), BF),
            pltpu.VMEM((nq, tok, HEAD_DIM), BF),
            pltpu.VMEM((HEADS, tok, HEAD_DIM), BF),
            pltpu.VMEM(w_out.shape, BF),
            pltpu.VMEM((1, d), F32),
            pltpu.VMEM((1, d), F32),
            pltpu.VMEM(w_final.shape[::-1], BF),
            pltpu.VMEM(conv_weight.shape, BF),
            pltpu.VMEM((tok, PICKS * tok), BF),
            pltpu.VMEM((4 * LATENT_CH, PICKS * 128), BF),
            pltpu.VMEM((tok, d), F32),
            pltpu.VMEM((n, tok // n, 128), F32),
            pltpu.VMEM((n, tok // n, 128), F32),
            dma((3,)), dma((2,)), dma((nq,)), dma((HEADS,)), dma((1,)), dma((5,)),
        ],
        compiler_params=pltpu.CompilerParams(
            collective_id=0, has_side_effects=True, vmem_limit_bytes=32 * 1024 * 1024
        ),
        name="fused",
    )(
        *(
            pltpu.with_memory_space_constraint(x, pltpu.HBM)
            for x in (
                queries, keys, values, w_out,
                shift_mod.reshape(1, d), scale_mod.reshape(1, d), w_final.T, conv_weight,
            )
        )
    )
    return pl.pallas_call(
        conv_kernel,
        out_shape=jax.ShapeDtypeStruct((FRAMES, 2, 2 * ROWS, out_ch), BF),
        in_specs=[vm, vm, vm],
        out_specs=vm,
        scratch_shapes=[pltpu.VMEM((FRAMES * 2 * ROWS, 128), F32)] * 2,
        compiler_params=pltpu.CompilerParams(vmem_limit_bytes=8 * 1024 * 1024),
        name="conv",
    )(got, big_w, conv_bias.reshape(1, out_ch))


def solution(mesh):
    placed = (
        P(("groups", "seq"), None),
        P(("groups", "seq"), None),
        P(("groups", "seq"), None),
        P(),
        P("groups"),
        P("groups"),
        P(),
        P(),
        P(),
    )
    return jax.shard_map(
        shards,
        mesh=mesh,
        in_specs=placed,
        out_specs=P("groups", "seq", None, None),
        check_vma=False,
    )
```

```python
import functools
import math

import jax
import jax.numpy as jnp
from jax import lax
from jax.experimental import pallas as pl
from jax.experimental.pallas import tpu as pltpu
from jax.sharding import PartitionSpec as P

HEADS = 12
HEAD_DIM = 128
QUAD = 4
OWNERS = 3
CHUNK = 2048
PICKS = 5
LATENT_CH = 16
FRAMES = 4
ROWS = 32
BF = jnp.bfloat16
F32 = jnp.float32


def mm(a, b):
    return lax.dot_general(a, b, (((1,), (0,)), ((), ())), preferred_element_type=F32)


def iota(shape, dim):
    return lax.broadcasted_iota(jnp.int32, shape, dim)


def ones_where(cond):
    return jnp.where(cond, 1.0, 0.0).astype(BF)


def kernel(
    n, split,
    q_hbm, k_hbm, v_hbm, w_out_hbm, shift_hbm, scale_hbm, w_final_hbm, conv_hbm,
    out_ref, big_w,
    qb, kb, vb, ob, att, w_out_v, shift_v, scale_v, w_final_v, conv_v, row_picks, ch_picks, proj, send_b, recv_b,
    s_send, kv_recv, q_recv, o_recv, e_recv, loc,
):
    me = lax.axis_index("seq")
    grp = me // QUAD
    tok = q_hbm.shape[0]
    rows_dev = tok // n
    groups = n // QUAD
    nq = n // split
    quads = nq // QUAD

    def cols(h):
        return pl.ds(pl.multiple_of(h * HEAD_DIM, 128), HEAD_DIM)

    def remote(src, dst, ssem, rsem, dev):
        return pltpu.make_async_remote_copy(
            src_ref=src, dst_ref=dst, send_sem=ssem, recv_sem=rsem,
            device_id={"seq": dev}, device_id_type=pl.DeviceIdType.MESH,
        )

    def arrived(ref, sem):
        pltpu.make_async_copy(ref, ref, sem).wait()

    def place(g, p):
        return g * QUAD + (p + 2 * (g % 2)) % QUAD

    mine = (me % QUAD + QUAD - 2 * (grp % 2)) % QUAD
    unit = grp * OWNERS + mine
    head = unit // split
    origin = (unit % split) * nq

    barrier = pltpu.get_barrier_semaphore()

    def greet(i, c):
        pl.semaphore_signal(
            barrier, inc=1, device_id={"seq": me ^ (n - 1 - i)}, device_id_type=pl.DeviceIdType.MESH
        )
        return c

    lax.fori_loop(0, n - 1, greet, 0)
    pl.semaphore_wait(barrier, n - 1)

    raw = (q_hbm, k_hbm, v_hbm)
    bufs = (qb, kb, vb)

    def target(i, swap):
        g = grp ^ (groups - 1 - i // OWNERS)
        g = jnp.where(swap & (i // OWNERS < 2), g ^ 1, g)
        p = i % OWNERS
        return g * OWNERS + p, place(g, p)

    def push(t, u, dev):
        src = raw[t].at[:, cols(u // split)]
        slot = me % nq if t == 0 else me
        sem = q_recv.at[slot] if t == 0 else kv_recv.at[t - 1]

        @pl.when(dev != me)
        def _():
            remote(src, bufs[t].at[slot], s_send.at[0], sem, dev).start()

        @pl.when(dev == me)
        def _():
            pltpu.make_async_copy(src, bufs[t].at[slot], sem).start()

    def push_kv(i, c):
        u, dev = target(i, True)
        push(1, u, dev)
        push(2, u, dev)
        return c

    def push_q(i, c):
        u, dev = target(i, False)

        @pl.when(u % split == me // nq)
        def _():
            push(0, u, dev)

        return c

    lax.fori_loop(0, groups * OWNERS, push_kv, 0)
    lax.fori_loop(0, groups * OWNERS, push_q, 0)
    loads = [
        pltpu.make_async_copy(src, dst, loc.at[i])
        for i, (src, dst) in enumerate(
            ((w_out_hbm, w_out_v), (shift_hbm, shift_v), (scale_hbm, scale_v), (w_final_hbm, w_final_v), (conv_hbm, conv_v))
        )
    ]
    for c in loads[::-1]:
        c.start()

    ch = iota((4 * LATENT_CH, 128), 0)
    lane = iota((4 * LATENT_CH, 128), 1)
    base = 4 * (lane % 16) + 2 * (lane // 64)
    xcol = (lane // 16) % 4
    row = iota((tok, tok), 0)
    col = iota((tok, tok), 1)
    w = row // rows_dev
    here = (row % rows_dev) * n + w
    picks = (
        ((col == here - 1) & (w > 0), (xcol == 0) & (ch == base + 1)),
        ((col == here) & (w == 0), (xcol == 0) & (ch == base)),
        (col == here, ((xcol == 1) & (ch == base)) | ((xcol == 2) & (ch == base + 1))),
        ((col == here + 1) & (w < n - 1), (xcol == 3) & (ch == base)),
        ((col == here) & (w == n - 1), (xcol == 3) & (ch == base + 1)),
    )
    for i, (rows_pick, ch_pick) in enumerate(picks):
        row_picks[:, i * tok : (i + 1) * tok] = ones_where(rows_pick)
        ch_picks[:, i * 128 : (i + 1) * 128] = ones_where(ch_pick)
    loads[-1].wait()
    spread_weights(conv_v, big_w)

    def near_order(i, quads):
        z = grp % quads
        outer = (z % 2) == (z // (quads // 2))
        return z ^ jnp.where(outer & (i > 1), i ^ 1, i)

    factor = math.log2(math.e) / math.sqrt(HEAD_DIM)
    keys = n * tok
    chunk = min(keys, CHUNK)
    pair = 2 * tok

    def scores(qh, c):
        kh = kb[pl.ds(c * (chunk // tok), chunk // tok)].reshape(chunk, HEAD_DIM)
        s = lax.dot_general(qh, kh, (((1,), (1,)), ((), ())), preferred_element_type=F32)
        return s * factor

    def weigh(s, top, c):
        vh = vb[pl.ds(c * (chunk // tok), chunk // tok)].reshape(chunk, HEAD_DIM)
        p = jnp.exp2(s - top).astype(BF)
        return mm(p, jnp.concatenate([vh, jnp.ones((chunk, HEAD_DIM), BF)], axis=1))

    def attend(i, carry):
        slot = QUAD * near_order(i // 2, quads) + 2 * (i % 2)
        for e in range(2):
            arrived(qb.at[slot + e], q_recv.at[slot + e])
        qh = qb[pl.ds(slot, 2)].reshape(pair, HEAD_DIM)
        if chunk == keys:
            s = scores(qh, 0)
            acc = weigh(s, jnp.max(s, axis=1, keepdims=True), 0)
        else:

            def step(c, state):
                top, acc = state
                s = scores(qh, c)
                new = jnp.maximum(top, jnp.max(s, axis=1, keepdims=True))
                return new, acc * jnp.exp2(top - new) + weigh(s, new, c)

            first = jnp.full((pair, 1), -1e30, F32), jnp.zeros((pair, 2 * HEAD_DIM), F32)
            acc = lax.fori_loop(0, keys // chunk, step, first)[1]
        ob[pl.ds(slot, 2)] = (acc[:, :HEAD_DIM] / acc[:, HEAD_DIM:]).astype(BF).reshape(2, tok, HEAD_DIM)
        for e in range(2):
            dev = origin + slot + e

            @pl.when(dev != me)
            def _(e=e, dev=dev):
                remote(ob.at[slot + e], att.at[head], s_send.at[1], o_recv.at[head], dev).start()

            @pl.when(dev == me)
            def _(e=e):
                pltpu.make_async_copy(ob.at[slot + e], att.at[head], o_recv.at[head]).start()

        return carry

    @pl.when(mine < OWNERS)
    def _():
        arrived(kb, kv_recv.at[0])
        arrived(vb, kv_recv.at[1])
        lax.fori_loop(0, nq // 2, attend, 0)

    for c in loads[:-1]:
        c.wait()
    half = HEADS // 2
    mine_first = (grp % (HEADS // OWNERS)) // 2
    for i in range(2):
        first = half * ((mine_first + i) % 2)
        for e in range(half):
            arrived(att.at[first + e], o_recv.at[first + e])
        lhs = jnp.concatenate([att[first + e] for e in range(half)], axis=1)
        rows = pl.ds(pl.multiple_of(first * HEAD_DIM, half * HEAD_DIM), half * HEAD_DIM)
        term = mm(lhs, w_out_v[rows])
        proj[...] = term if i == 0 else proj[...] + term
    projected = proj[...]
    centered = projected - jnp.mean(projected, axis=1, keepdims=True)
    variance = jnp.mean(centered * centered, axis=1, keepdims=True)
    normed = (
        centered * lax.rsqrt(variance + 1e-06) * (1.0 + scale_v[...]) + shift_v[...]
    ).astype(BF)
    patches = lax.dot_general(
        normed, w_final_v[...], (((1,), (1,)), ((), ())), preferred_element_type=F32
    ).astype(BF)

    spread = mm(patches, ch_picks[...]).astype(BF)
    window = mm(
        row_picks[...], jnp.concatenate([spread[:, i * 128 : (i + 1) * 128] for i in range(PICKS)], axis=0)
    )
    send_b[...] = window.reshape(n, rows_dev, 128)

    def exchange(i, c):
        dev = me ^ (n - 1 - i)
        remote(send_b.at[dev], recv_b.at[me], s_send.at[2], e_recv.at[0], dev).start()
        return c

    lax.fori_loop(0, n - 1, exchange, 0)
    recv_b[me] = send_b[me]
    owner = mine < OWNERS
    units = groups * OWNERS
    gone = (
        (units - 1, 0, ~owner),
        (units - 1, 0, ~owner),
        (HEADS - 1, 0, ~(owner & (unit % split == me // nq))),
    )
    for count, sem, one_more in gone:
        arrived(kb.at[pl.ds(0, count)], s_send.at[sem])

        @pl.when(one_more)
        def _(sem=sem):
            arrived(kb.at[0], s_send.at[sem])

    @pl.when(owner)
    def _():
        arrived(ob.at[pl.ds(0, nq - 1)], s_send.at[1])

        @pl.when(origin // nq != me // nq)
        def _():
            arrived(ob.at[0], s_send.at[1])

    arrived(recv_b.at[pl.ds(0, n - 1)], e_recv.at[0])
    arrived(send_b.at[pl.ds(0, n - 1)], s_send.at[2])
    out_ref[...] = recv_b[...].reshape(out_ref.shape)


def spread_weights(conv_v, big_w):
    out_ch = conv_v.shape[1]
    big_w[...] = jnp.zeros(big_w.shape, BF)
    for a in range(3):
        for e in range(3):
            for b in range(3):
                for s in range(2):
                    row = a * 256 + e * 64 + (b + s) * 16
                    tap = (9 * a + 3 * b + e) * 16
                    big_w[row : row + 16, s * out_ch : (s + 1) * out_ch] = conv_v[tap : tap + 16, :]


def conv_kernel(got_ref, big_w, bias_ref, out_ref, left, right):
    out_ch = bias_ref.shape[1]
    cells = FRAMES * ROWS
    got = got_ref[...]
    turned = pltpu.roll(got, 64, 1)
    low = iota(got.shape, 1) < 64
    row = iota(got.shape, 0) % ROWS
    above = jnp.where(row == 0, got, pltpu.roll(turned, 1, 0))
    below = jnp.where(row == ROWS - 1, turned, pltpu.roll(got, cells - 1, 0))
    left[pl.ds(0, cells, 2), :] = jnp.where(low, above, turned)
    right[pl.ds(0, cells, 2), :] = jnp.where(low, turned, 0.0)
    left[pl.ds(1, cells, 2), :] = got
    right[pl.ds(1, cells, 2), :] = jnp.where(low, below, 0.0)
    taps = jnp.concatenate([left[...], right[...]], axis=1).astype(BF)
    frames = [taps[f * 2 * ROWS : (f + 1) * 2 * ROWS] for f in range(FRAMES)]
    feats = jnp.concatenate(
        [jnp.concatenate([frames[max(f + a - 2, 0)] for f in range(FRAMES)], axis=0) for a in range(3)], axis=1
    )
    for s in range(2):
        res = mm(feats, big_w[:, s * out_ch : (s + 1) * out_ch]) + bias_ref[...]
        res = res.astype(BF)
        for f in range(FRAMES):
            out_ref[f, s] = res[f * 2 * ROWS : (f + 1) * 2 * ROWS]


def shards(queries, keys, values, w_out, shift_mod, scale_mod, w_final, conv_weight, conv_bias):
    n = lax.axis_size("seq")
    split = n * OWNERS // (QUAD * HEADS)
    tok = queries.shape[0]
    d = w_out.shape[1]
    out_ch = conv_weight.shape[1]
    vm = pl.BlockSpec(memory_space=pltpu.VMEM)
    hbm = pl.BlockSpec(memory_space=pltpu.HBM)
    dma = pltpu.SemaphoreType.DMA
    nq = n // split
    got, big_w = pl.pallas_call(
        functools.partial(kernel, n, split),
        out_shape=(
            jax.ShapeDtypeStruct((FRAMES * ROWS, 128), F32),
            jax.ShapeDtypeStruct((768, 2 * out_ch), BF),
        ),
        in_specs=[hbm] * 8,
        out_specs=(vm, vm),
        scratch_shapes=[
            pltpu.VMEM((nq, tok, HEAD_DIM), BF),
            pltpu.VMEM((n, tok, HEAD_DIM), BF),
            pltpu.VMEM((n, tok, HEAD_DIM), BF),
            pltpu.VMEM((nq, tok, HEAD_DIM), BF),
            pltpu.VMEM((HEADS, tok, HEAD_DIM), BF),
            pltpu.VMEM(w_out.shape, BF),
            pltpu.VMEM((1, d), F32),
            pltpu.VMEM((1, d), F32),
            pltpu.VMEM(w_final.shape[::-1], BF),
            pltpu.VMEM(conv_weight.shape, BF),
            pltpu.VMEM((tok, PICKS * tok), BF),
            pltpu.VMEM((4 * LATENT_CH, PICKS * 128), BF),
            pltpu.VMEM((tok, d), F32),
            pltpu.VMEM((n, tok // n, 128), F32),
            pltpu.VMEM((n, tok // n, 128), F32),
            dma((3,)), dma((2,)), dma((nq,)), dma((HEADS,)), dma((1,)), dma((5,)),
        ],
        compiler_params=pltpu.CompilerParams(
            collective_id=0, has_side_effects=True, vmem_limit_bytes=32 * 1024 * 1024
        ),
        name="fused",
    )(
        *(
            pltpu.with_memory_space_constraint(x, pltpu.HBM)
            for x in (
                queries, keys, values, w_out,
                shift_mod.reshape(1, d), scale_mod.reshape(1, d), w_final.T, conv_weight,
            )
        )
    )
    return pl.pallas_call(
        conv_kernel,
        out_shape=jax.ShapeDtypeStruct((FRAMES, 2, 2 * ROWS, out_ch), BF),
        in_specs=[vm, vm, vm],
        out_specs=vm,
        scratch_shapes=[pltpu.VMEM((FRAMES * 2 * ROWS, 128), F32)] * 2,
        compiler_params=pltpu.CompilerParams(vmem_limit_bytes=8 * 1024 * 1024),
        name="conv",
    )(got, big_w, conv_bias.reshape(1, out_ch))


def solution(mesh):
    placed = (
        P(("groups", "seq"), None),
        P(("groups", "seq"), None),
        P(("groups", "seq"), None),
        P(),
        P("groups"),
        P("groups"),
        P(),
        P(),
        P(),
    )
    return jax.shard_map(
        shards,
        mesh=mesh,
        in_specs=placed,
        out_specs=P("groups", "seq", None, None),
        check_vma=False,
    )
```

```python
import functools
import math

import jax
import jax.numpy as jnp
from jax import lax
from jax.experimental import pallas as pl
from jax.experimental.pallas import tpu as pltpu
from jax.sharding import PartitionSpec as P

HEADS = 12
HEAD_DIM = 128
QUAD = 4
OWNERS = 3
CHUNK = 2048
PICKS = 5
LATENT_CH = 16
FRAMES = 4
ROWS = 32
BF = jnp.bfloat16
F32 = jnp.float32


def mm(a, b):
    return lax.dot_general(a, b, (((1,), (0,)), ((), ())), preferred_element_type=F32)


def iota(shape, dim):
    return lax.broadcasted_iota(jnp.int32, shape, dim)


def ones_where(cond):
    return jnp.where(cond, 1.0, 0.0).astype(BF)


def kernel(
    n, split,
    q_hbm, k_hbm, v_hbm, w_out_hbm, shift_hbm, scale_hbm, w_final_hbm, conv_hbm,
    out_ref, big_w,
    qb, kb, vb, ob, att, w_out_v, shift_v, scale_v, w_final_v, conv_v, row_picks, ch_picks, proj, send_b, recv_b,
    s_send, kv_recv, q_recv, o_recv, e_recv, loc,
):
    me = lax.axis_index("seq")
    grp = me // QUAD
    tok = q_hbm.shape[0]
    rows_dev = tok // n
    groups = n // QUAD
    nq = n // split
    quads = nq // QUAD

    def cols(h):
        return pl.ds(pl.multiple_of(h * HEAD_DIM, 128), HEAD_DIM)

    def remote(src, dst, ssem, rsem, dev):
        return pltpu.make_async_remote_copy(
            src_ref=src, dst_ref=dst, send_sem=ssem, recv_sem=rsem,
            device_id={"seq": dev}, device_id_type=pl.DeviceIdType.MESH,
        )

    def arrived(ref, sem):
        pltpu.make_async_copy(ref, ref, sem).wait()

    def place(g, p):
        return g * QUAD + (p + 2 * (g % 2)) % QUAD

    mine = (me % QUAD + QUAD - 2 * (grp % 2)) % QUAD
    unit = grp * OWNERS + mine
    head = unit // split
    origin = (unit % split) * nq

    barrier = pltpu.get_barrier_semaphore()

    def greet(i, c):
        pl.semaphore_signal(
            barrier, inc=1, device_id={"seq": me ^ (n - 1 - i)}, device_id_type=pl.DeviceIdType.MESH
        )
        return c

    lax.fori_loop(0, n - 1, greet, 0)
    pl.semaphore_wait(barrier, n - 1)

    raw = (q_hbm, k_hbm, v_hbm)
    bufs = (qb, kb, vb)

    def target(i, swap):
        g = grp ^ (groups - 1 - i // OWNERS)
        g = jnp.where(swap & (i // OWNERS < 2), g ^ 1, g)
        p = i % OWNERS
        return g * OWNERS + p, place(g, p)

    def push(t, u, dev):
        src = raw[t].at[:, cols(u // split)]
        slot = me % nq if t == 0 else me
        sem = q_recv.at[slot] if t == 0 else kv_recv.at[t - 1]

        @pl.when(dev != me)
        def _():
            remote(src, bufs[t].at[slot], s_send.at[0], sem, dev).start()

        @pl.when(dev == me)
        def _():
            pltpu.make_async_copy(src, bufs[t].at[slot], sem).start()

    def push_kv(i, c):
        u, dev = target(i, True)
        push(1, u, dev)
        push(2, u, dev)
        return c

    def push_q(i, c):
        u, dev = target(i, False)

        @pl.when(u % split == me // nq)
        def _():
            push(0, u, dev)

        return c

    lax.fori_loop(0, groups * OWNERS, push_kv, 0)
    lax.fori_loop(0, groups * OWNERS, push_q, 0)
    loads = [
        pltpu.make_async_copy(src, dst, loc.at[i])
        for i, (src, dst) in enumerate(
            ((w_out_hbm, w_out_v), (shift_hbm, shift_v), (scale_hbm, scale_v), (w_final_hbm, w_final_v), (conv_hbm, conv_v))
        )
    ]
    for c in loads[::-1]:
        c.start()

    ch = iota((4 * LATENT_CH, 128), 0)
    lane = iota((4 * LATENT_CH, 128), 1)
    base = 4 * (lane % 16) + 2 * (lane // 64)
    xcol = (lane // 16) % 4
    row = iota((tok, tok), 0)
    col = iota((tok, tok), 1)
    w = row // rows_dev
    here = (row % rows_dev) * n + w
    picks = (
        ((col == here - 1) & (w > 0), (xcol == 0) & (ch == base + 1)),
        ((col == here) & (w == 0), (xcol == 0) & (ch == base)),
        (col == here, ((xcol == 1) & (ch == base)) | ((xcol == 2) & (ch == base + 1))),
        ((col == here + 1) & (w < n - 1), (xcol == 3) & (ch == base)),
        ((col == here) & (w == n - 1), (xcol == 3) & (ch == base + 1)),
    )
    for i, (rows_pick, ch_pick) in enumerate(picks):
        row_picks[:, i * tok : (i + 1) * tok] = ones_where(rows_pick)
        ch_picks[:, i * 128 : (i + 1) * 128] = ones_where(ch_pick)
    loads[-1].wait()
    spread_weights(conv_v, big_w)

    def near_order(i, quads):
        z = grp % quads
        outer = (z % 2) == (z // (quads // 2))
        return z ^ jnp.where(outer & (i > 1), i ^ 1, i)

    factor = math.log2(math.e) / math.sqrt(HEAD_DIM)
    keys = n * tok
    chunk = min(keys, CHUNK)
    pair = 2 * tok

    def scores(qh, c):
        kh = kb[pl.ds(c * (chunk // tok), chunk // tok)].reshape(chunk, HEAD_DIM)
        s = lax.dot_general(qh, kh, (((1,), (1,)), ((), ())), preferred_element_type=F32)
        return s * factor

    def weigh(s, top, c):
        vh = vb[pl.ds(c * (chunk // tok), chunk // tok)].reshape(chunk, HEAD_DIM)
        p = jnp.exp2(s - top).astype(BF)
        return mm(p, jnp.concatenate([vh, jnp.ones((chunk, HEAD_DIM), BF)], axis=1))

    def attend(i, carry):
        slot = QUAD * near_order(i // 2, quads) + 2 * ((i + me // 2) % 2)
        for e in range(2):
            arrived(qb.at[slot + e], q_recv.at[slot + e])
        qh = qb[pl.ds(slot, 2)].reshape(pair, HEAD_DIM)
        if chunk == keys:
            s = scores(qh, 0)
            acc = weigh(s, jnp.max(s, axis=1, keepdims=True), 0)
        else:

            def step(c, state):
                top, acc = state
                s = scores(qh, c)
                new = jnp.maximum(top, jnp.max(s, axis=1, keepdims=True))
                return new, acc * jnp.exp2(top - new) + weigh(s, new, c)

            first = jnp.full((pair, 1), -1e30, F32), jnp.zeros((pair, 2 * HEAD_DIM), F32)
            acc = lax.fori_loop(0, keys // chunk, step, first)[1]
        ob[pl.ds(slot, 2)] = (acc[:, :HEAD_DIM] / acc[:, HEAD_DIM:]).astype(BF).reshape(2, tok, HEAD_DIM)
        for e in range(2):
            dev = origin + slot + e

            @pl.when(dev != me)
            def _(e=e, dev=dev):
                remote(ob.at[slot + e], att.at[head], s_send.at[1], o_recv.at[head], dev).start()

            @pl.when(dev == me)
            def _(e=e):
                pltpu.make_async_copy(ob.at[slot + e], att.at[head], o_recv.at[head]).start()

        return carry

    @pl.when(mine < OWNERS)
    def _():
        arrived(kb, kv_recv.at[0])
        arrived(vb, kv_recv.at[1])
        lax.fori_loop(0, nq // 2, attend, 0)

    for c in loads[:-1]:
        c.wait()
    half = HEADS // 2
    mine_first = (grp % (HEADS // OWNERS)) // 2
    for i in range(2):
        first = half * ((mine_first + i) % 2)
        for e in range(half):
            arrived(att.at[first + e], o_recv.at[first + e])
        lhs = jnp.concatenate([att[first + e] for e in range(half)], axis=1)
        rows = pl.ds(pl.multiple_of(first * HEAD_DIM, half * HEAD_DIM), half * HEAD_DIM)
        term = mm(lhs, w_out_v[rows])
        proj[...] = term if i == 0 else proj[...] + term
    projected = proj[...]
    centered = projected - jnp.mean(projected, axis=1, keepdims=True)
    variance = jnp.mean(centered * centered, axis=1, keepdims=True)
    normed = (
        centered * lax.rsqrt(variance + 1e-06) * (1.0 + scale_v[...]) + shift_v[...]
    ).astype(BF)
    patches = lax.dot_general(
        normed, w_final_v[...], (((1,), (1,)), ((), ())), preferred_element_type=F32
    ).astype(BF)

    spread = mm(patches, ch_picks[...]).astype(BF)
    window = mm(
        row_picks[...], jnp.concatenate([spread[:, i * 128 : (i + 1) * 128] for i in range(PICKS)], axis=0)
    )
    send_b[...] = window.reshape(n, rows_dev, 128)

    def exchange(i, c):
        dev = me ^ (n - 1 - i)
        remote(send_b.at[dev], recv_b.at[me], s_send.at[2], e_recv.at[0], dev).start()
        return c

    lax.fori_loop(0, n - 1, exchange, 0)
    recv_b[me] = send_b[me]
    owner = mine < OWNERS
    units = groups * OWNERS
    gone = (
        (units - 1, 0, ~owner),
        (units - 1, 0, ~owner),
        (HEADS - 1, 0, ~(owner & (unit % split == me // nq))),
    )
    for count, sem, one_more in gone:
        arrived(kb.at[pl.ds(0, count)], s_send.at[sem])

        @pl.when(one_more)
        def _(sem=sem):
            arrived(kb.at[0], s_send.at[sem])

    @pl.when(owner)
    def _():
        arrived(ob.at[pl.ds(0, nq - 1)], s_send.at[1])

        @pl.when(origin // nq != me // nq)
        def _():
            arrived(ob.at[0], s_send.at[1])

    arrived(recv_b.at[pl.ds(0, n - 1)], e_recv.at[0])
    arrived(send_b.at[pl.ds(0, n - 1)], s_send.at[2])
    out_ref[...] = recv_b[...].reshape(out_ref.shape)


def spread_weights(conv_v, big_w):
    out_ch = conv_v.shape[1]
    big_w[...] = jnp.zeros(big_w.shape, BF)
    for a in range(3):
        for e in range(3):
            for b in range(3):
                for s in range(2):
                    row = a * 256 + e * 64 + (b + s) * 16
                    tap = (9 * a + 3 * b + e) * 16
                    big_w[row : row + 16, s * out_ch : (s + 1) * out_ch] = conv_v[tap : tap + 16, :]


def conv_kernel(got_ref, big_w, bias_ref, out_hbm, left, right, out_v, sem):
    out_ch = bias_ref.shape[1]
    cells = FRAMES * ROWS
    got = got_ref[...]
    turned = pltpu.roll(got, 64, 1)
    low = iota(got.shape, 1) < 64
    row = iota(got.shape, 0) % ROWS
    above = jnp.where(row == 0, got, pltpu.roll(turned, 1, 0))
    below = jnp.where(row == ROWS - 1, turned, pltpu.roll(got, cells - 1, 0))
    left[pl.ds(0, cells, 2), :] = jnp.where(low, above, turned)
    right[pl.ds(0, cells, 2), :] = jnp.where(low, turned, 0.0)
    left[pl.ds(1, cells, 2), :] = got
    right[pl.ds(1, cells, 2), :] = jnp.where(low, below, 0.0)
    taps = jnp.concatenate([left[...], right[...]], axis=1).astype(BF)
    frames = [taps[f * 2 * ROWS : (f + 1) * 2 * ROWS] for f in range(FRAMES)]
    feats = jnp.concatenate(
        [jnp.concatenate([frames[max(f + a - 2, 0)] for f in range(FRAMES)], axis=0) for a in range(3)], axis=1
    )
    writes = []
    for s in range(2):
        res = mm(feats, big_w[:, s * out_ch : (s + 1) * out_ch]) + bias_ref[...]
        out_v[s] = res.astype(BF).reshape(FRAMES, 2 * ROWS, out_ch)
        writes.append(pltpu.make_async_copy(out_v.at[s], out_hbm.at[:, s], sem.at[s]))
        writes[-1].start()
    for c in writes:
        c.wait()


def shards(queries, keys, values, w_out, shift_mod, scale_mod, w_final, conv_weight, conv_bias):
    n = lax.axis_size("seq")
    split = n * OWNERS // (QUAD * HEADS)
    tok = queries.shape[0]
    d = w_out.shape[1]
    out_ch = conv_weight.shape[1]
    vm = pl.BlockSpec(memory_space=pltpu.VMEM)
    hbm = pl.BlockSpec(memory_space=pltpu.HBM)
    dma = pltpu.SemaphoreType.DMA
    nq = n // split
    got, big_w = pl.pallas_call(
        functools.partial(kernel, n, split),
        out_shape=(
            jax.ShapeDtypeStruct((FRAMES * ROWS, 128), F32),
            jax.ShapeDtypeStruct((768, 2 * out_ch), BF),
        ),
        in_specs=[hbm] * 8,
        out_specs=(vm, vm),
        scratch_shapes=[
            pltpu.VMEM((nq, tok, HEAD_DIM), BF),
            pltpu.VMEM((n, tok, HEAD_DIM), BF),
            pltpu.VMEM((n, tok, HEAD_DIM), BF),
            pltpu.VMEM((nq, tok, HEAD_DIM), BF),
            pltpu.VMEM((HEADS, tok, HEAD_DIM), BF),
            pltpu.VMEM(w_out.shape, BF),
            pltpu.VMEM((1, d), F32),
            pltpu.VMEM((1, d), F32),
            pltpu.VMEM(w_final.shape[::-1], BF),
            pltpu.VMEM(conv_weight.shape, BF),
            pltpu.VMEM((tok, PICKS * tok), BF),
            pltpu.VMEM((4 * LATENT_CH, PICKS * 128), BF),
            pltpu.VMEM((tok, d), F32),
            pltpu.VMEM((n, tok // n, 128), F32),
            pltpu.VMEM((n, tok // n, 128), F32),
            dma((3,)), dma((2,)), dma((nq,)), dma((HEADS,)), dma((1,)), dma((5,)),
        ],
        compiler_params=pltpu.CompilerParams(
            collective_id=0, has_side_effects=True, vmem_limit_bytes=32 * 1024 * 1024
        ),
        name="fused",
    )(
        *(
            pltpu.with_memory_space_constraint(x, pltpu.HBM)
            for x in (
                queries, keys, values, w_out,
                shift_mod.reshape(1, d), scale_mod.reshape(1, d), w_final.T, conv_weight,
            )
        )
    )
    return pl.pallas_call(
        conv_kernel,
        out_shape=jax.ShapeDtypeStruct((FRAMES, 2, 2 * ROWS, out_ch), BF),
        in_specs=[vm, vm, vm],
        out_specs=hbm,
        scratch_shapes=[pltpu.VMEM((FRAMES * 2 * ROWS, 128), F32)] * 2
        + [pltpu.VMEM((2, FRAMES, 2 * ROWS, out_ch), BF), dma((2,))],
        compiler_params=pltpu.CompilerParams(vmem_limit_bytes=8 * 1024 * 1024),
        name="conv",
    )(got, big_w, conv_bias.reshape(1, out_ch))


def solution(mesh):
    placed = (
        P(("groups", "seq"), None),
        P(("groups", "seq"), None),
        P(("groups", "seq"), None),
        P(),
        P("groups"),
        P("groups"),
        P(),
        P(),
        P(),
    )
    return jax.shard_map(
        shards,
        mesh=mesh,
        in_specs=placed,
        out_specs=P("groups", "seq", None, None),
        check_vma=False,
    )
```

```python
import functools
import math

import jax
import jax.numpy as jnp
from jax import lax
from jax.experimental import pallas as pl
from jax.experimental.pallas import tpu as pltpu
from jax.sharding import PartitionSpec as P

HEADS = 12
HEAD_DIM = 128
QUAD = 4
OWNERS = 3
CHUNK = 2048
PICKS = 5
LATENT_CH = 16
FRAMES = 4
ROWS = 32
BF = jnp.bfloat16
F32 = jnp.float32


def mm(a, b):
    return lax.dot_general(a, b, (((1,), (0,)), ((), ())), preferred_element_type=F32)


def iota(shape, dim):
    return lax.broadcasted_iota(jnp.int32, shape, dim)


def ones_where(cond):
    return jnp.where(cond, 1.0, 0.0).astype(BF)


def kernel(
    n, split,
    q_hbm, k_hbm, v_hbm, w_out_hbm, shift_hbm, scale_hbm, w_final_hbm, conv_hbm,
    out_ref, big_w,
    qb, kb, vb, ob, att, w_out_v, shift_v, scale_v, w_final_v, conv_v, w_turned, row_picks, ch_picks, proj, send_b, recv_b,
    s_send, kv_recv, q_recv, o_recv, e_recv, loc,
):
    me = lax.axis_index("seq")
    grp = me // QUAD
    tok = q_hbm.shape[0]
    rows_dev = tok // n
    groups = n // QUAD
    nq = n // split
    quads = nq // QUAD

    def cols(h):
        return pl.ds(pl.multiple_of(h * HEAD_DIM, 128), HEAD_DIM)

    def remote(src, dst, ssem, rsem, dev):
        return pltpu.make_async_remote_copy(
            src_ref=src, dst_ref=dst, send_sem=ssem, recv_sem=rsem,
            device_id={"seq": dev}, device_id_type=pl.DeviceIdType.MESH,
        )

    def arrived(ref, sem):
        pltpu.make_async_copy(ref, ref, sem).wait()

    def place(g, p):
        return g * QUAD + (p + 2 * (g % 2)) % QUAD

    mine = (me % QUAD + QUAD - 2 * (grp % 2)) % QUAD
    unit = grp * OWNERS + mine
    head = unit // split
    origin = (unit % split) * nq

    barrier = pltpu.get_barrier_semaphore()

    def greet(i, c):
        pl.semaphore_signal(
            barrier, inc=1, device_id={"seq": me ^ (n - 1 - i)}, device_id_type=pl.DeviceIdType.MESH
        )
        return c

    lax.fori_loop(0, n - 1, greet, 0)
    pl.semaphore_wait(barrier, n - 1)

    raw = (q_hbm, k_hbm, v_hbm)
    bufs = (qb, kb, vb)

    def target(i, swap):
        g = grp ^ (groups - 1 - i // OWNERS)
        g = jnp.where(swap & (i // OWNERS < 2), g ^ 1, g)
        p = i % OWNERS
        return g * OWNERS + p, place(g, p)

    def push(t, u, dev):
        src = raw[t].at[:, cols(u // split)]
        slot = me % nq if t == 0 else me
        sem = q_recv.at[slot] if t == 0 else kv_recv.at[t - 1]

        @pl.when(dev != me)
        def _():
            remote(src, bufs[t].at[slot], s_send.at[0], sem, dev).start()

        @pl.when(dev == me)
        def _():
            pltpu.make_async_copy(src, bufs[t].at[slot], sem).start()

    def push_kv(i, c):
        u, dev = target(i, True)
        push(1, u, dev)
        push(2, u, dev)
        return c

    def push_q(i, c):
        u, dev = target(i, False)

        @pl.when(u % split == me // nq)
        def _():
            push(0, u, dev)

        return c

    lax.fori_loop(0, groups * OWNERS, push_kv, 0)
    lax.fori_loop(0, groups * OWNERS, push_q, 0)
    loads = [
        pltpu.make_async_copy(src, dst, loc.at[i])
        for i, (src, dst) in enumerate(
            ((w_out_hbm, w_out_v), (shift_hbm, shift_v), (scale_hbm, scale_v), (w_final_hbm, w_final_v), (conv_hbm, conv_v))
        )
    ]
    for c in loads[::-1]:
        c.start()

    ch = iota((4 * LATENT_CH, 128), 0)
    lane = iota((4 * LATENT_CH, 128), 1)
    base = 4 * (lane % 16) + 2 * (lane // 64)
    xcol = (lane // 16) % 4
    row = iota((tok, tok), 0)
    col = iota((tok, tok), 1)
    w = row // rows_dev
    here = (row % rows_dev) * n + w
    picks = (
        ((col == here - 1) & (w > 0), (xcol == 0) & (ch == base + 1)),
        ((col == here) & (w == 0), (xcol == 0) & (ch == base)),
        (col == here, ((xcol == 1) & (ch == base)) | ((xcol == 2) & (ch == base + 1))),
        ((col == here + 1) & (w < n - 1), (xcol == 3) & (ch == base)),
        ((col == here) & (w == n - 1), (xcol == 3) & (ch == base + 1)),
    )
    for i, (rows_pick, ch_pick) in enumerate(picks):
        row_picks[:, i * tok : (i + 1) * tok] = ones_where(rows_pick)
        ch_picks[:, i * 128 : (i + 1) * 128] = ones_where(ch_pick)
    loads[-1].wait()
    loads[-2].wait()
    w_turned[...] = w_final_v[...].T
    spread_weights(conv_v, big_w)

    def near_order(i, quads):
        z = grp % quads
        outer = (z % 2) == (z // (quads // 2))
        return z ^ jnp.where(outer & (i > 1), i ^ 1, i)

    factor = math.log2(math.e) / math.sqrt(HEAD_DIM)
    keys = n * tok
    chunk = min(keys, CHUNK)
    pair = 2 * tok

    def scores(qh, c):
        kh = kb[pl.ds(c * (chunk // tok), chunk // tok)].reshape(chunk, HEAD_DIM)
        s = lax.dot_general(qh, kh, (((1,), (1,)), ((), ())), preferred_element_type=F32)
        return s * factor

    def weigh(s, top, c):
        vh = vb[pl.ds(c * (chunk // tok), chunk // tok)].reshape(chunk, HEAD_DIM)
        p = jnp.exp2(s - top).astype(BF)
        return mm(p, jnp.concatenate([vh, jnp.ones((chunk, HEAD_DIM), BF)], axis=1))

    def attend(i, carry):
        slot = QUAD * near_order(i // 2, quads) + 2 * ((i + me // 2) % 2)
        for e in range(2):
            arrived(qb.at[slot + e], q_recv.at[slot + e])
        qh = qb[pl.ds(slot, 2)].reshape(pair, HEAD_DIM)
        if chunk == keys:
            s = scores(qh, 0)
            acc = weigh(s, jnp.max(s, axis=1, keepdims=True), 0)
        else:

            def step(c, state):
                top, acc = state
                s = scores(qh, c)
                new = jnp.maximum(top, jnp.max(s, axis=1, keepdims=True))
                return new, acc * jnp.exp2(top - new) + weigh(s, new, c)

            first = jnp.full((pair, 1), -1e30, F32), jnp.zeros((pair, 2 * HEAD_DIM), F32)
            acc = lax.fori_loop(0, keys // chunk, step, first)[1]
        ob[pl.ds(slot, 2)] = (acc[:, :HEAD_DIM] / acc[:, HEAD_DIM:]).astype(BF).reshape(2, tok, HEAD_DIM)
        for e in range(2):
            dev = origin + slot + e

            @pl.when(dev != me)
            def _(e=e, dev=dev):
                remote(ob.at[slot + e], att.at[head], s_send.at[1], o_recv.at[head], dev).start()

            @pl.when(dev == me)
            def _(e=e):
                pltpu.make_async_copy(ob.at[slot + e], att.at[head], o_recv.at[head]).start()

        return carry

    @pl.when(mine < OWNERS)
    def _():
        arrived(kb, kv_recv.at[0])
        arrived(vb, kv_recv.at[1])
        lax.fori_loop(0, nq // 2, attend, 0)

    for c in loads[:-2]:
        c.wait()
    half = HEADS // 2
    mine_first = (grp % (HEADS // OWNERS)) // 2
    for i in range(2):
        first = half * ((mine_first + i) % 2)
        for e in range(half):
            arrived(att.at[first + e], o_recv.at[first + e])
        lhs = jnp.concatenate([att[first + e] for e in range(half)], axis=1)
        rows = pl.ds(pl.multiple_of(first * HEAD_DIM, half * HEAD_DIM), half * HEAD_DIM)
        term = mm(lhs, w_out_v[rows])
        proj[...] = term if i == 0 else proj[...] + term
    projected = proj[...]
    centered = projected - jnp.mean(projected, axis=1, keepdims=True)
    variance = jnp.mean(centered * centered, axis=1, keepdims=True)
    normed = (
        centered * lax.rsqrt(variance + 1e-06) * (1.0 + scale_v[...]) + shift_v[...]
    ).astype(BF)
    patches = mm(normed, w_turned[...]).astype(BF)
    spread = mm(patches, ch_picks[...]).astype(BF)
    window = mm(
        row_picks[...], jnp.concatenate([spread[:, i * 128 : (i + 1) * 128] for i in range(PICKS)], axis=0)
    )
    send_b[...] = window.reshape(n, rows_dev, 128)

    def exchange(i, c):
        dev = me ^ (n - 1 - i)
        remote(send_b.at[dev], recv_b.at[me], s_send.at[2], e_recv.at[0], dev).start()
        return c

    lax.fori_loop(0, n - 1, exchange, 0)
    recv_b[me] = send_b[me]
    owner = mine < OWNERS
    units = groups * OWNERS
    gone = (
        (units - 1, 0, ~owner),
        (units - 1, 0, ~owner),
        (HEADS - 1, 0, ~(owner & (unit % split == me // nq))),
    )
    for count, sem, one_more in gone:
        arrived(kb.at[pl.ds(0, count)], s_send.at[sem])

        @pl.when(one_more)
        def _(sem=sem):
            arrived(kb.at[0], s_send.at[sem])

    @pl.when(owner)
    def _():
        arrived(ob.at[pl.ds(0, nq - 1)], s_send.at[1])

        @pl.when(origin // nq != me // nq)
        def _():
            arrived(ob.at[0], s_send.at[1])

    arrived(recv_b.at[pl.ds(0, n - 1)], e_recv.at[0])
    arrived(send_b.at[pl.ds(0, n - 1)], s_send.at[2])
    out_ref[...] = recv_b[...].reshape(out_ref.shape)


def spread_weights(conv_v, big_w):
    out_ch = conv_v.shape[1]
    big_w[...] = jnp.zeros(big_w.shape, BF)
    for a in range(3):
        for e in range(3):
            for b in range(3):
                for s in range(2):
                    row = a * 256 + e * 64 + (b + s) * 16
                    tap = (9 * a + 3 * b + e) * 16
                    big_w[row : row + 16, s * out_ch : (s + 1) * out_ch] = conv_v[tap : tap + 16, :]


def conv_kernel(got_ref, big_w, bias_ref, out_hbm, left, right, out_v, sem):
    out_ch = bias_ref.shape[1]
    cells = FRAMES * ROWS
    got = got_ref[...]
    turned = pltpu.roll(got, 64, 1)
    low = iota(got.shape, 1) < 64
    row = iota(got.shape, 0) % ROWS
    above = jnp.where(row == 0, got, pltpu.roll(turned, 1, 0))
    below = jnp.where(row == ROWS - 1, turned, pltpu.roll(got, cells - 1, 0))
    left[pl.ds(0, cells, 2), :] = jnp.where(low, above, turned)
    right[pl.ds(0, cells, 2), :] = jnp.where(low, turned, 0.0)
    left[pl.ds(1, cells, 2), :] = got
    right[pl.ds(1, cells, 2), :] = jnp.where(low, below, 0.0)
    taps = jnp.concatenate([left[...], right[...]], axis=1).astype(BF)
    frames = [taps[f * 2 * ROWS : (f + 1) * 2 * ROWS] for f in range(FRAMES)]
    feats = jnp.concatenate(
        [jnp.concatenate([frames[max(f + a - 2, 0)] for f in range(FRAMES)], axis=0) for a in range(3)], axis=1
    )
    writes = []
    for s in range(2):
        res = mm(feats, big_w[:, s * out_ch : (s + 1) * out_ch]) + bias_ref[...]
        out_v[s] = res.astype(BF).reshape(FRAMES, 2 * ROWS, out_ch)
        writes.append(pltpu.make_async_copy(out_v.at[s], out_hbm.at[:, s], sem.at[s]))
        writes[-1].start()
    for c in writes:
        c.wait()


def shards(queries, keys, values, w_out, shift_mod, scale_mod, w_final, conv_weight, conv_bias):
    n = lax.axis_size("seq")
    split = n * OWNERS // (QUAD * HEADS)
    tok = queries.shape[0]
    d = w_out.shape[1]
    out_ch = conv_weight.shape[1]
    vm = pl.BlockSpec(memory_space=pltpu.VMEM)
    hbm = pl.BlockSpec(memory_space=pltpu.HBM)
    dma = pltpu.SemaphoreType.DMA
    nq = n // split
    got, big_w = pl.pallas_call(
        functools.partial(kernel, n, split),
        out_shape=(
            jax.ShapeDtypeStruct((FRAMES * ROWS, 128), F32),
            jax.ShapeDtypeStruct((768, 2 * out_ch), BF),
        ),
        in_specs=[hbm] * 8,
        out_specs=(vm, vm),
        scratch_shapes=[
            pltpu.VMEM((nq, tok, HEAD_DIM), BF),
            pltpu.VMEM((n, tok, HEAD_DIM), BF),
            pltpu.VMEM((n, tok, HEAD_DIM), BF),
            pltpu.VMEM((nq, tok, HEAD_DIM), BF),
            pltpu.VMEM((HEADS, tok, HEAD_DIM), BF),
            pltpu.VMEM(w_out.shape, BF),
            pltpu.VMEM((1, d), F32),
            pltpu.VMEM((1, d), F32),
            pltpu.VMEM(w_final.shape[::-1], BF),
            pltpu.VMEM(conv_weight.shape, BF),
            pltpu.VMEM(w_final.shape, BF),
            pltpu.VMEM((tok, PICKS * tok), BF),
            pltpu.VMEM((4 * LATENT_CH, PICKS * 128), BF),
            pltpu.VMEM((tok, d), F32),
            pltpu.VMEM((n, tok // n, 128), F32),
            pltpu.VMEM((n, tok // n, 128), F32),
            dma((3,)), dma((2,)), dma((nq,)), dma((HEADS,)), dma((1,)), dma((5,)),
        ],
        compiler_params=pltpu.CompilerParams(
            collective_id=0, has_side_effects=True, vmem_limit_bytes=32 * 1024 * 1024
        ),
        name="fused",
    )(
        *(
            pltpu.with_memory_space_constraint(x, pltpu.HBM)
            for x in (
                queries, keys, values, w_out,
                shift_mod.reshape(1, d), scale_mod.reshape(1, d), w_final.T, conv_weight,
            )
        )
    )
    return pl.pallas_call(
        conv_kernel,
        out_shape=jax.ShapeDtypeStruct((FRAMES, 2, 2 * ROWS, out_ch), BF),
        in_specs=[vm, vm, vm],
        out_specs=hbm,
        scratch_shapes=[pltpu.VMEM((FRAMES * 2 * ROWS, 128), F32)] * 2
        + [pltpu.VMEM((2, FRAMES, 2 * ROWS, out_ch), BF), dma((2,))],
        compiler_params=pltpu.CompilerParams(vmem_limit_bytes=8 * 1024 * 1024),
        name="conv",
    )(got, big_w, conv_bias.reshape(1, out_ch))


def solution(mesh):
    placed = (
        P(("groups", "seq"), None),
        P(("groups", "seq"), None),
        P(("groups", "seq"), None),
        P(),
        P("groups"),
        P("groups"),
        P(),
        P(),
        P(),
    )
    return jax.shard_map(
        shards,
        mesh=mesh,
        in_specs=placed,
        out_specs=P("groups", "seq", None, None),
        check_vma=False,
    )
```
